128 devices in a mesh: row: 8 (over x, z_lo), col: 16 (over z_hi, y, core).
Axes of the slice: x: 4, y: 4, z: 4 (z_hi: 2, z_lo: 2; z = z_hi * 2 + z_lo), core: 2. Of those that a mesh axis runs over, the one named last changes fastest.
Arguments:
- pixels: bfloat16 [64, 64000, 144], P(None, ('row', 'col')), may hold values from 0.049804688 to 4
- match_filter: bfloat16 [64000, 2, 144], P(('row', 'col')), may hold values from -48 to 48
- tile_ranks: int32 [64, 256], P('row', 'col'), may hold values from 1 to 64
- column_order: int32 [256], replicated, may hold values from 0 to 255, each once
- right_factors: bfloat16 [64, 256, 64, 500], P('row', 'col'), may hold values from -0.25 to 0.25
- left_factors: bfloat16 [64, 256, 64, 500], P('row', 'col'), may hold values from -0.046875 to 0.046875
Outputs:
- commands: float32 [64, 32000], P(None, ('row', 'col'))
The draws below stay inside these ranges and needn't reach their ends.
Inputs may be any that keep to these rules, and one draw needn't show every extreme that they name: `column_order`: every slope block is read by exactly one tile column.
All inputs are finite; a program needn't handle non-finite values.
Results may differ from the reference program's by a relative error of at most 0.0041.
Values may be sent and summed in bfloat16 or wider, within the bound.
A program may use at most 128 MiB of HBM per device.

```python
import math
import jax
import jax.numpy as jnp
from jax import lax

PIX = 144
TILE = 500
RMAX = 64
FRAMES = 64
TCOLS = 256
TROWS = 64
SUBAPS = 64000
SLOPES = 128000
ACT = 32000


def touch_ends(values, stream_key, low, high):
    longest = values.shape.index(max(values.shape))
    spots = []
    for shift in (0, 1):
        where = [jax.random.randint(jax.random.fold_in(stream_key, axis), (), 0, length) for axis, length in enumerate(values.shape)]
        where[longest] = (where[longest] + shift) % values.shape[longest]
        spots.append(tuple(where))
    return values.at[spots[0]].set(low).at[spots[1]].set(high)


def steps_of(rng, extent, shards, smallest, largest):
    level, own = 1.0, jax.random.fold_in(rng, 6)
    for dim, blocks in shards:
        steps = jnp.exp(jax.random.uniform(jax.random.fold_in(own, dim), (blocks,), jnp.float32, smallest / len(shards), largest / len(shards)))
        level = level * jnp.repeat(steps, extent[dim] // blocks).reshape([-1 if axis == dim else 1 for axis in range(len(extent))])
    return level


def scatter_about(rng, extent, deviation, limit, cuts=(), kind=jnp.bfloat16):
    factor_of = steps_of(rng, extent, cuts, -0.22, 0.18) if cuts else 1.0
    result = jax.random.normal(rng, extent, jnp.float32) * deviation * factor_of
    return jnp.minimum(jnp.maximum(result, -limit), limit).astype(kind)


def setup_inputs(seed: int = 0) -> dict:
    keys = jax.random.split(jax.random.key(seed), 7)
    return {
        "pixels": jnp.clip(jnp.exp(math.log(4.0) - 4.3859405 * jax.random.uniform(keys[0], (FRAMES, SUBAPS, PIX), jnp.float32) ** steps_of(keys[0], (FRAMES, SUBAPS, PIX), ((1, 128),), -0.2, 0.2)), 0.049804688, 4.0).astype(jnp.bfloat16),
        "match_filter": scatter_about(keys[1], (SUBAPS, 2, PIX), 8.0, 48.0, ((0, 128),)),
        "tile_ranks": touch_ends(jax.random.randint(keys[2], (TROWS, TCOLS), 1, RMAX + 1), jax.random.fold_in(keys[2], 1), 1, RMAX).astype(jnp.int32),
        "column_order": jax.random.permutation(keys[3], TCOLS).astype(jnp.int32),
        "right_factors": scatter_about(keys[4], (TROWS, TCOLS, RMAX, TILE), TILE ** -0.5, 0.25, ((0, 8), (1, 16))),
        "left_factors": scatter_about(keys[5], (TROWS, TCOLS, RMAX, TILE), (RMAX * TCOLS) ** -0.5, 0.046875, ((0, 8), (1, 16))),
    }


def reference(pixels, match_filter, tile_ranks, column_order, right_factors, left_factors):
    filters_wide = match_filter.astype(jnp.float32)

    def centroid(frame_pixels):
        values = frame_pixels.astype(jnp.float32)
        flux = jnp.sum(values, axis=1)
        raw = jnp.einsum('sp,skp->sk', values, filters_wide)
        return (raw / flux[:, None]).astype(jnp.bfloat16).reshape(SLOPES)

    slopes = lax.map(centroid, pixels)
    blocks = slopes.reshape(FRAMES, TCOLS, TILE)
    picked = jnp.take(blocks, column_order, axis=1).astype(jnp.float32)
    component = jnp.arange(RMAX, dtype=jnp.int32)

    def tile_row(inputs):
        right_row, left_row, rank_row = inputs
        projection = jnp.einsum('jkt,fjt->jkf', right_row.astype(jnp.float32), picked)
        keep = component[None, :] < rank_row[:, None]
        projection = jnp.where(keep[:, :, None], projection, 0.0).astype(jnp.bfloat16)
        return jnp.einsum('jkf,jka->fa', projection.astype(jnp.float32), left_row.astype(jnp.float32))

    rows_out = lax.map(tile_row, (right_factors, left_factors, tile_ranks))
    return jnp.transpose(rows_out, (1, 0, 2)).reshape(FRAMES, ACT)
```

```python
import jax
import jax.numpy as jnp
from jax import lax
from jax.experimental import pallas as pl
from jax.experimental.pallas import tpu as pltpu
from jax.sharding import PartitionSpec as P

BF16 = jnp.bfloat16
F32 = jnp.float32
ROWS, COLS = 8, 16
FRAMES, SUBS, PIX = 64, 500, 144
TILE, RANK = 500, 64
SPAN_I, SPAN_J = 8, 16
HALF = 250
PIX_CHUNKS = 8
CHUNK_FRAMES = FRAMES // PIX_CHUNKS
R_CHUNKS = 4
R_COLS = SPAN_J // R_CHUNKS
GATHER_CHUNKS = 4
PAIRS = SPAN_J // 2
CHUNK_PAIRS = PAIRS // GATHER_CHUNKS


def one_hot(shape, target_of_row):
    row = lax.broadcasted_iota(jnp.int32, shape, 0)
    col = lax.broadcasted_iota(jnp.int32, shape, 1)
    return jnp.where(col == target_of_row(row), 1.0, 0.0).astype(BF16)


def permute(matrix, rows):
    return jnp.dot(matrix, rows, preferred_element_type=F32).astype(BF16)


def kernel(
    order_ref, ranks_ref, pix_hbm, filt_hbm, right_hbm, left_hbm, out_ref,
    pix, filt, filt32, right, left, slopes, sel, by_row, from_row, by_mid, at_mid, by_col, from_col,
    mine_u, gathered, proj, other_half, my_half, half_in, chunk_out, chunk_in,
    filt_sem, pix_sem, right_sem, left_sem,
    a1_send, a1_recv, a2_send, a2_recv, a3_send, a3_recv, b_send, b_recv,
    c1_send, c1_recv, c2_send, c2_recv,
):
    r = lax.axis_index("row")
    c = lax.axis_index("col")
    group = c // 2
    core = c % 2

    def row_peer(d):
        return lax.rem(r + d, ROWS)

    def col_peer(d):
        return lax.rem(c + d, COLS)

    def pix_copy(n):
        frames = pl.ds(n * CHUNK_FRAMES, CHUNK_FRAMES)
        return pltpu.make_async_copy(pix_hbm.at[frames], pix.at[frames], pix_sem.at[n])

    def right_copy(n):
        cols = pl.ds(n * R_COLS, R_COLS)
        return pltpu.make_async_copy(right_hbm.at[:, cols], right.at[:, cols], right_sem.at[n])

    def left_copy(n):
        return pltpu.make_async_copy(left_hbm.at[n], left.at[n], left_sem.at[n])

    filt_copy = pltpu.make_async_copy(filt_hbm, filt, filt_sem)
    filt_copy.start()
    for n in range(PIX_CHUNKS):
        pix_copy(n).start()
    for n in range(R_CHUNKS):
        right_copy(n).start()
    for n in range(SPAN_I):
        left_copy(n).start()

    barrier = pltpu.get_barrier_semaphore()
    for d in range(1, ROWS):
        pl.semaphore_signal(barrier, inc=1, device_id={"row": row_peer(d)}, device_id_type=pl.DeviceIdType.MESH)
    for d in range(1, COLS):
        pl.semaphore_signal(barrier, inc=1, device_id={"col": col_peer(d)}, device_id_type=pl.DeviceIdType.MESH)

    row_z = lax.broadcasted_iota(jnp.int32, (256, 256), 0)
    block_of_row = ((row_z >> 1) & 7) * 32 + (row_z >> 4) * 2 + (row_z & 1)
    sel[...] = jnp.where(block_of_row == order_ref[...], 1.0, 0.0).T.astype(BF16)
    slopes[...] = jnp.zeros_like(slopes)

    filt_copy.wait()
    filt32[...] = filt[...].astype(F32)

    def centroid(n, carry):
        pix_copy(n).wait()
        for lane in range(4):
            low, high = lane * 128, min(lane * 128 + 128, SUBS)
            width = high - low

            def add(p, sums):
                rows = pl.ds(pl.multiple_of(p * 16, 16), 16)
                fx = filt32[0, rows, low:high]
                fy = filt32[1, rows, low:high]
                new = []
                for f in range(CHUNK_FRAMES):
                    v = pix[n * CHUNK_FRAMES + f, rows, low:high].astype(F32)
                    vx, vy = v * fx, v * fy
                    s, sx, sy = sums[3 * f : 3 * f + 3]
                    new += [s + (v[:8] + v[8:]), sx + (vx[:8] + vx[8:]), sy + (vy[:8] + vy[8:])]
                return tuple(new)

            zero = jnp.zeros((8, width), F32)
            sums = lax.fori_loop(0, PIX // 16, add, (zero,) * (3 * CHUNK_FRAMES))

            def total(kind):
                return jnp.concatenate(
                    [jnp.sum(sums[3 * f + kind], axis=0, keepdims=True) for f in range(CHUNK_FRAMES)], axis=0
                )

            flux = total(0)
            frames = pl.ds(pl.multiple_of(n * CHUNK_FRAMES, 8), CHUNK_FRAMES)
            slopes[0, frames, low:high] = total(1) / flux
            slopes[1, frames, low:high] = total(2) / flux
        return carry

    lax.fori_loop(0, PIX_CHUNKS, centroid, 0)

    parts = []
    for b in range(2):
        kinds = [slopes[k] if b == 0 else pltpu.roll(slopes[k], 512 - HALF, 1) for k in range(2)]
        for h in range(2):
            parts.append(jnp.concatenate([v[:, h * 128 : h * 128 + 128] for v in kinds], axis=1))
    raw = jnp.concatenate(parts, axis=0).astype(BF16)
    lanes = one_hot((256, 256), lambda row: (row & 127) * 2 + (row >> 7))
    order_rows = one_hot(
        (256, 256), lambda row: (row & 1) * 128 + ((row >> 4) & 1) * 64 + (row >> 5) * 8 + ((row >> 1) & 7)
    )
    by_row[...] = permute(order_rows, permute(raw, lanes)).reshape(ROWS, 32, 256)

    pl.semaphore_wait(barrier, ROWS - 1 + COLS - 1)

    def remote(src, dst, send, recv, device):
        return pltpu.make_async_remote_copy(
            src_ref=src, dst_ref=dst, send_sem=send, recv_sem=recv,
            device_id=device, device_id_type=pl.DeviceIdType.MESH,
        )

    a1 = [
        remote(by_row.at[row_peer(d)], from_row.at[r], a1_send.at[d - 1], a1_recv.at[d - 1], {"row": row_peer(d)})
        for d in range(1, ROWS)
    ]
    for copy in a1:
        copy.start()
    from_row[r] = by_row[r]
    middle = one_hot((256, 256), lambda row: ((row >> 1) & 7) * 32 + (row >> 4) * 2 + (row & 1))
    for copy in a1:
        copy.wait_recv()
    by_mid[...] = permute(middle, from_row[...].reshape(256, 256)).reshape(COLS, 16, 256)

    a2 = [
        remote(by_mid.at[col_peer(d)], at_mid.at[c], a2_send.at[d - 1], a2_recv.at[d - 1], {"col": col_peer(d)})
        for d in range(1, COLS)
    ]
    for copy in a2:
        copy.start()
    at_mid[c] = by_mid[c]
    for copy in a2:
        copy.wait_recv()
    by_col[...] = permute(sel[...], at_mid[...].reshape(256, 256)).reshape(COLS, 16, 256)

    a3 = [
        remote(by_col.at[col_peer(d)], from_col.at[c], a3_send.at[d - 1], a3_recv.at[d - 1], {"col": col_peer(d)})
        for d in range(1, COLS)
    ]
    for copy in a3:
        copy.start()
    from_col[c] = by_col[c]
    frame_rows = one_hot((128, 128), lambda row: (row & 7) * 16 + (row >> 3))
    for copy in a3:
        copy.wait_recv()
    for h in range(2):
        piece = from_col[h * 8 : h * 8 + 8].reshape(128, 256)
        mine_u[:, :, h * 256 : h * 256 + 256] = permute(frame_rows, piece).reshape(PAIRS, 16, 256)

    def gather_copy(n, d):
        pairs = pl.ds(n * CHUNK_PAIRS, CHUNK_PAIRS)
        return remote(
            mine_u.at[pairs], gathered.at[r, pairs], b_send.at[n, d - 1], b_recv.at[n, d - 1], {"row": row_peer(d)}
        )

    for n in range(GATHER_CHUNKS):
        for d in range(1, ROWS):
            gather_copy(n, d).start()
    gathered[r] = mine_u[...]

    lane_id = lax.broadcasted_iota(jnp.int32, (FRAMES, 128), 1)
    low_half = lane_id < RANK
    component = lane_id & (RANK - 1)

    def project(n, carry):
        right_copy(n).wait()
        for d in range(1, ROWS):
            gather_copy(n, d).wait_recv()
        for q in range(CHUNK_PAIRS):
            pair = n * CHUNK_PAIRS + q
            both = gathered[:, pair].astype(F32)
            halves = []
            for e in range(2):
                piece = both[:, e * 8 : e * 8 + 8, :].reshape(FRAMES, 512).astype(BF16)
                factors = right[:, 2 * pair + e].reshape(SPAN_I * RANK, TILE)
                halves.append(
                    lax.dot_general(
                        piece[:, :TILE], factors, (((1,), (1,)), ((), ())), preferred_element_type=F32
                    )
                )
            for i2 in range(SPAN_I // 2):
                kept = []
                for e in range(2):
                    bound = jnp.where(
                        low_half, ranks_ref[2 * i2, 2 * pair + e], ranks_ref[2 * i2 + 1, 2 * pair + e]
                    )
                    kept.append(jnp.where(component < bound, halves[e][:, i2 * 128 : i2 * 128 + 128], 0.0))
                proj[2 * i2, pair] = jnp.where(low_half, kept[0], pltpu.roll(kept[1], RANK, 1)).astype(BF16)
                proj[2 * i2 + 1, pair] = jnp.where(low_half, pltpu.roll(kept[0], RANK, 1), kept[1]).astype(BF16)
        return carry

    lax.fori_loop(0, GATHER_CHUNKS, project, 0)

    for n in range(SPAN_I):
        left_copy(n).wait()

    def half_copy(s):
        return remote(
            other_half.at[s], half_in.at[s], c1_send.at[s], c1_recv.at[s], {"col": c + 1 - 2 * core}
        )

    def tile_of(s):
        return lax.rem(group + 1 + s, SPAN_I)

    def chunk_copy(s):
        return remote(
            chunk_out.at[s], chunk_in.at[s], c2_send.at[s], c2_recv.at[s], {"col": 2 * tile_of(s) + core}
        )

    def finish(s):
        half_copy(s).wait_recv()
        chunk_out[s] = (my_half[s] + half_in[s]).astype(BF16)
        chunk_copy(s).start()

    def command(s, carry):
        i = tile_of(s)
        lhs = jnp.concatenate([proj[i, q] for q in range(PAIRS)], axis=1)
        full = jnp.dot(lhs, left[i].reshape(SPAN_J * RANK, TILE), preferred_element_type=F32)
        lower, upper = full[:, :HALF], full[:, HALF:]
        first = core == 0
        my_half[s] = jnp.where(first, lower, upper)
        other_half[s] = jnp.where(first, upper, lower)
        half_copy(s).start()

        @pl.when(s >= 1)
        def _():
            finish(s - 1)

        return carry

    lax.fori_loop(0, SPAN_I, command, 0)
    last = SPAN_I - 1
    half_copy(last).wait_recv()
    total_cmd = my_half[last] + half_in[last]
    for s in range(last):
        chunk_copy(s).wait_recv()
        total_cmd += chunk_in[s].astype(F32)
    out_ref[...] = total_cmd

    for copy in a1 + a2 + a3:
        copy.wait_send()
    for n in range(GATHER_CHUNKS):
        for d in range(1, ROWS):
            gather_copy(n, d).wait_send()
    for s in range(SPAN_I):
        half_copy(s).wait_send()
    for s in range(last):
        chunk_copy(s).wait_send()


def shards(pixels, match_filter, tile_ranks, column_order, right_factors, left_factors):
    hbm = pl.BlockSpec(memory_space=pl.ANY)
    dma = pltpu.SemaphoreType.DMA
    return pl.pallas_call(
        kernel,
        out_shape=jax.ShapeDtypeStruct((FRAMES, HALF), F32),
        in_specs=[
            pl.BlockSpec(memory_space=pltpu.VMEM),
            pl.BlockSpec(memory_space=pltpu.SMEM),
            hbm, hbm, hbm, hbm,
        ],
        out_specs=pl.BlockSpec(memory_space=pltpu.VMEM),
        scratch_shapes=[
            pltpu.VMEM((FRAMES, PIX, SUBS), BF16),
            pltpu.VMEM((2, PIX, SUBS), BF16),
            pltpu.VMEM((2, PIX, SUBS), F32),
            pltpu.VMEM((SPAN_I, SPAN_J, RANK, TILE), BF16),
            pltpu.VMEM((SPAN_I, SPAN_J, RANK, TILE), BF16),
            pltpu.VMEM((2, FRAMES, 512), F32),
            pltpu.VMEM((256, 256), BF16),
            pltpu.VMEM((ROWS, 32, 256), BF16),
            pltpu.VMEM((ROWS, 32, 256), BF16),
            pltpu.VMEM((COLS, 16, 256), BF16),
            pltpu.VMEM((COLS, 16, 256), BF16),
            pltpu.VMEM((COLS, 16, 256), BF16),
            pltpu.VMEM((COLS, 16, 256), BF16),
            pltpu.VMEM((PAIRS, 16, 512), BF16),
            pltpu.VMEM((ROWS, PAIRS, 16, 512), BF16),
            pltpu.VMEM((SPAN_I, PAIRS, FRAMES, 128), BF16),
            pltpu.VMEM((SPAN_I, FRAMES, HALF), F32),
            pltpu.VMEM((SPAN_I, FRAMES, HALF), F32),
            pltpu.VMEM((SPAN_I, FRAMES, HALF), F32),
            pltpu.VMEM((SPAN_I - 1, FRAMES, HALF), BF16),
            pltpu.VMEM((SPAN_I - 1, FRAMES, HALF), BF16),
            dma, dma((PIX_CHUNKS,)), dma((R_CHUNKS,)), dma((SPAN_I,)),
            dma((ROWS - 1,)), dma((ROWS - 1,)),
            dma((COLS - 1,)), dma((COLS - 1,)),
            dma((COLS - 1,)), dma((COLS - 1,)),
            dma((GATHER_CHUNKS, ROWS - 1)), dma((GATHER_CHUNKS, ROWS - 1)),
            dma((SPAN_I,)), dma((SPAN_I,)),
            dma((SPAN_I - 1,)), dma((SPAN_I - 1,)),
        ],
        compiler_params=pltpu.CompilerParams(
            collective_id=0, has_side_effects=True, vmem_limit_bytes=48 * 1024 * 1024
        ),
        name="frames_to_commands",
    )(
        column_order.reshape(1, -1),
        tile_ranks,
        jnp.transpose(pixels, (0, 2, 1)),
        jnp.transpose(match_filter, (1, 2, 0)),
        right_factors,
        left_factors,
    )


def solution(mesh):
    in_specs = (
        P(None, ("row", "col"), None),
        P(("row", "col"), None, None),
        P("row", "col"),
        P(),
        P("row", "col", None, None),
        P("row", "col", None, None),
    )
    out_specs = P(None, ("row", "col"))
    return jax.shard_map(shards, mesh=mesh, in_specs=in_specs, out_specs=out_specs, check_vma=False)
```

```python
import jax
import jax.numpy as jnp
from jax import lax
from jax.experimental import pallas as pl
from jax.experimental.pallas import tpu as pltpu
from jax.sharding import PartitionSpec as P

BF16 = jnp.bfloat16
F32 = jnp.float32
ROWS, COLS = 8, 16
FRAMES, SUBS, PIX = 64, 500, 144
TILE, RANK = 500, 64
SPAN_I, SPAN_J = 8, 16
HALF = 250
PIX_CHUNKS = 8
CHUNK_FRAMES = FRAMES // PIX_CHUNKS
R_CHUNKS = 4
R_COLS = SPAN_J // R_CHUNKS
PAIRS = SPAN_J // 2
CHUNK_PAIRS = PAIRS // R_CHUNKS
DEVICES = ROWS * COLS
MESH = pl.DeviceIdType.MESH


def one_hot(shape, target_of_row):
    row = lax.broadcasted_iota(jnp.int32, shape, 0)
    col = lax.broadcasted_iota(jnp.int32, shape, 1)
    return jnp.where(col == target_of_row(row), 1.0, 0.0).astype(BF16)


def permute(matrix, rows):
    return jnp.dot(matrix, rows, preferred_element_type=F32).astype(BF16)


def kernel(
    order_hbm, ranks_hbm, pix_hbm, filt_hbm, right_hbm, left_hbm, out_ref,
    order, ranks, pix, filt, filt32, right, left, slopes, sel, lanes, frame_rows, rows32, by_piece, at_mid, by_col, gathered,
    pieces, proj, other_half, my_half, half_in, chunk_out, chunk_in,
    order_sem, ranks_sem, filt_sem, pix_sem, right_sem, left_sem,
    spread_send, spread_recv, gather_send, gather_recv,
    c1_send, c1_recv, c2_send, c2_recv,
):
    r = lax.axis_index("row")
    c = lax.axis_index("col")
    core = lax.rem(c, 2)
    y = lax.rem(c // 2, 4)
    z_hi = c // 8
    x = r // 2
    z = z_hi * 2 + lax.rem(r, 2)
    rank = r * COLS + c

    xs = [lax.rem(x + d, 4) for d in range(4)]
    ys = [lax.rem(y + d, 4) for d in range(4)]
    zs = [lax.rem(z + d, 4) for d in range(4)]
    cores = [core, 1 - core]
    offsets = [(dx, dy, dz, dk) for dx in range(4) for dy in range(4) for dz in range(4) for dk in range(2)]
    offsets.sort(key=lambda o: -sum(min(d, 4 - d) for d in o[:3]))
    peers = [
        (xs[dx] * 2 + lax.rem(zs[dz], 2), (zs[dz] // 2 * 4 + ys[dy]) * 2 + cores[dk])
        for dx, dy, dz, dk in offsets
        if (dx, dy, dz, dk) != (0, 0, 0, 0)
    ]

    def pix_copy(n):
        frames = pl.ds(n * CHUNK_FRAMES, CHUNK_FRAMES)
        return pltpu.make_async_copy(pix_hbm.at[frames], pix.at[frames], pix_sem.at[n])

    def right_copy(n):
        cols = pl.ds(n * R_COLS, R_COLS)
        return pltpu.make_async_copy(right_hbm.at[:, cols], right.at[:, cols], right_sem.at[n])

    def left_copy(n):
        return pltpu.make_async_copy(left_hbm.at[n], left.at[n], left_sem.at[n])

    order_copy = pltpu.make_async_copy(order_hbm, order, order_sem)
    ranks_copy = pltpu.make_async_copy(ranks_hbm, ranks, ranks_sem)
    filt_copy = pltpu.make_async_copy(filt_hbm, filt, filt_sem)
    filt_copy.start()
    order_copy.start()
    ranks_copy.start()
    for n in range(PIX_CHUNKS):
        pix_copy(n).start()
    barrier = pltpu.get_barrier_semaphore()
    for row, col in peers:
        pl.semaphore_signal(barrier, inc=1, device_id={"row": row, "col": col}, device_id_type=MESH)

    order_copy.wait()
    wanted = jnp.broadcast_to(order[...].astype(F32), (128, 256)).T
    source = lax.broadcasted_iota(jnp.int32, (256, 128), 1)
    for b in range(2):
        match = (source * 2 + b).astype(F32) == wanted
        sel[:, b * 128 : b * 128 + 128] = jnp.where(match, 1.0, 0.0).astype(BF16)
    lanes[...] = one_hot((256, 256), lambda row: (row & 127) * 2 + (row >> 7))
    frame_rows[...] = one_hot((256, 256), lambda row: (row & 15) * 16 + (row >> 4))
    rows32[...] = jnp.zeros_like(rows32)
    slopes[...] = jnp.zeros_like(slopes)

    filt_copy.wait()
    filt32[...] = filt[...].astype(F32)

    def centroid(n, carry):
        pix_copy(n).wait()
        for lane in range(4):
            low, high = lane * 128, min(lane * 128 + 128, SUBS)
            width = high - low

            def add(p, sums):
                rows = pl.ds(pl.multiple_of(p * 16, 16), 16)
                fx = filt32[0, rows, low:high]
                fy = filt32[1, rows, low:high]
                new = []
                for f in range(CHUNK_FRAMES):
                    v = pix[n * CHUNK_FRAMES + f, rows, low:high].astype(F32)
                    vx, vy = v * fx, v * fy
                    s, sx, sy = sums[3 * f : 3 * f + 3]
                    new += [s + (v[:8] + v[8:]), sx + (vx[:8] + vx[8:]), sy + (vy[:8] + vy[8:])]
                return tuple(new)

            zero = jnp.zeros((8, width), F32)
            sums = lax.fori_loop(0, PIX // 16, add, (zero,) * (3 * CHUNK_FRAMES))

            def total(kind):
                return jnp.concatenate(
                    [jnp.sum(sums[3 * f + kind], axis=0, keepdims=True) for f in range(CHUNK_FRAMES)], axis=0
                )

            flux = total(0)
            frames = pl.ds(pl.multiple_of(n * CHUNK_FRAMES, 8), CHUNK_FRAMES)
            slopes[0, frames, low:high] = total(1) / flux
            slopes[1, frames, low:high] = total(2) / flux
        return carry

    lax.fori_loop(0, PIX_CHUNKS, centroid, 0)

    parts = []
    for b in range(2):
        kinds = [slopes[k] if b == 0 else pltpu.roll(slopes[k], 512 - HALF, 1) for k in range(2)]
        for h in range(2):
            parts.append(jnp.concatenate([v[:, h * 128 : h * 128 + 128] for v in kinds], axis=1))
    raw = jnp.concatenate(parts, axis=0).astype(BF16)
    raw = jnp.dot(raw, lanes[...], preferred_element_type=F32)

    for b in range(2):
        for h in range(2):
            for q in range(2):
                first = b * 128 + h * 64
                rows32[pl.ds(h * 8 + b * 2 + q, FRAMES, stride=16), :] = raw[
                    first : first + FRAMES, q * 128 : q * 128 + 128
                ]
    by_piece[...] = rows32[...].reshape(DEVICES, 8, 128).astype(BF16)

    pl.semaphore_wait(barrier, DEVICES - 1)

    def remote(src, dst, send, recv, device):
        return pltpu.make_async_remote_copy(
            src_ref=src, dst_ref=dst, send_sem=send, recv_sem=recv, device_id=device, device_id_type=MESH
        )

    for row, col in peers:
        remote(
            by_piece.at[row * COLS + col], at_mid.at[rank], spread_send, spread_recv, {"row": row, "col": col}
        ).start()
    at_mid[rank] = by_piece[rank]
    for n in range(R_CHUNKS):
        right_copy(n).start()
    others = pl.ds(0, DEVICES - 1)
    spread = remote(by_piece.at[others], at_mid.at[others], spread_send, spread_recv, {"row": r})
    spread.wait_recv()
    rows32[...] = at_mid[...].astype(F32).reshape(DEVICES * 8, 128)
    every = jnp.concatenate(
        [
            jnp.concatenate([rows32[pl.ds(b * 2 + q, DEVICES, stride=8), :] for q in range(2)], axis=1)
            for b in range(2)
        ],
        axis=0,
    ).astype(BF16)
    by_col[...] = permute(sel[...], every).reshape(COLS, SPAN_J, 256)

    for row, col in peers:
        remote(by_col.at[col], gathered.at[rank], gather_send, gather_recv, {"row": row, "col": col}).start()
    gathered[rank] = by_col[c]
    for n in range(SPAN_I):
        left_copy(n).start()
    ranks_copy.wait()
    gather = remote(gathered.at[others], gathered.at[others], gather_send, gather_recv, {"row": r})
    gather.wait_recv()

    for g in range(FRAMES // 16):
        for h in range(2):
            rows = jnp.concatenate([gathered[2 * (g * 16 + f) + h] for f in range(16)], axis=0)
            pieces[:, g * 16 : g * 16 + 16, h * 256 : h * 256 + 256] = permute(frame_rows[...], rows).reshape(
                SPAN_J, 16, 256
            )

    lane_id = lax.broadcasted_iota(jnp.int32, (FRAMES, 128), 1)
    low_half = lane_id < RANK
    component = lane_id & (RANK - 1)

    def project(n, carry):
        right_copy(n).wait()
        for q in range(CHUNK_PAIRS):
            pair = n * CHUNK_PAIRS + q
            halves = []
            for e in range(2):
                piece = pieces[2 * pair + e]
                factors = right[:, 2 * pair + e].reshape(SPAN_I * RANK, TILE)
                halves.append(
                    lax.dot_general(
                        piece[:, :TILE], factors, (((1,), (1,)), ((), ())), preferred_element_type=F32
                    )
                )
            for i2 in range(SPAN_I // 2):
                kept = []
                for e in range(2):
                    bound = jnp.where(
                        low_half, ranks[2 * i2, 2 * pair + e], ranks[2 * i2 + 1, 2 * pair + e]
                    )
                    kept.append(jnp.where(component < bound, halves[e][:, i2 * 128 : i2 * 128 + 128], 0.0))
                proj[2 * i2, pair] = jnp.where(low_half, kept[0], pltpu.roll(kept[1], RANK, 1)).astype(BF16)
                proj[2 * i2 + 1, pair] = jnp.where(low_half, pltpu.roll(kept[0], RANK, 1), kept[1]).astype(BF16)
        return carry

    lax.fori_loop(0, R_CHUNKS, project, 0)

    for n in range(SPAN_I):
        left_copy(n).wait()

    def half_copy(s):
        return remote(
            other_half.at[s], half_in.at[s], c1_send.at[s], c1_recv.at[s], {"row": r, "col": c + 1 - 2 * core}
        )

    def tile_of(s):
        return lax.rem(z_hi + 1 - s // 4, 2) * 4 + lax.rem(y + 1 + s, 4)

    def chunk_copy(s):
        return remote(
            chunk_out.at[s], chunk_in.at[s], c2_send.at[s], c2_recv.at[s], {"row": r, "col": 2 * tile_of(s) + core}
        )

    def finish(s):
        half_copy(s).wait_recv()
        chunk_out[s] = (my_half[s] + half_in[s]).astype(BF16)
        chunk_copy(s).start()

    def command(s, carry):
        i = tile_of(s)
        lhs = jnp.concatenate([proj[i, q] for q in range(PAIRS)], axis=1)
        full = jnp.dot(lhs, left[i].reshape(SPAN_J * RANK, TILE), preferred_element_type=F32)
        lower, upper = full[:, :HALF], full[:, HALF:]
        first = core == 0
        my_half[s] = jnp.where(first, lower, upper)
        other_half[s] = jnp.where(first, upper, lower)
        half_copy(s).start()

        @pl.when(s >= 1)
        def _():
            finish(s - 1)

        return carry

    lax.fori_loop(0, SPAN_I, command, 0)
    last = SPAN_I - 1
    half_copy(last).wait_recv()
    total_cmd = my_half[last] + half_in[last]
    for s in range(last):
        chunk_copy(s).wait_recv()
        total_cmd += chunk_in[s].astype(F32)
    out_ref[...] = total_cmd

    spread.wait_send()
    gather.wait_send()
    for s in range(SPAN_I):
        half_copy(s).wait_send()
    for s in range(last):
        chunk_copy(s).wait_send()


def shards(pixels, match_filter, tile_ranks, column_order, right_factors, left_factors):
    hbm = pl.BlockSpec(memory_space=pltpu.HBM)
    dma = pltpu.SemaphoreType.DMA
    return pl.pallas_call(
        kernel,
        out_shape=jax.ShapeDtypeStruct((FRAMES, HALF), F32),
        in_specs=[hbm] * 6,
        out_specs=pl.BlockSpec(memory_space=pltpu.VMEM),
        scratch_shapes=[
            pltpu.VMEM((1, 256), jnp.int32),
            pltpu.SMEM((SPAN_I, SPAN_J), jnp.int32),
            pltpu.VMEM((FRAMES, PIX, SUBS), BF16),
            pltpu.VMEM((2, PIX, SUBS), BF16),
            pltpu.VMEM((2, PIX, SUBS), F32),
            pltpu.VMEM((SPAN_I, SPAN_J, RANK, TILE), BF16),
            pltpu.VMEM((SPAN_I, SPAN_J, RANK, TILE), BF16),
            pltpu.VMEM((2, FRAMES, 512), F32),
            pltpu.VMEM((256, 256), BF16),
            pltpu.VMEM((256, 256), BF16),
            pltpu.VMEM((256, 256), BF16),
            pltpu.VMEM((DEVICES * 8, 128), F32),
            pltpu.VMEM((DEVICES, 8, 128), BF16),
            pltpu.VMEM((DEVICES, 8, 128), BF16),
            pltpu.VMEM((COLS, SPAN_J, 256), BF16),
            pltpu.VMEM((DEVICES, SPAN_J, 256), BF16),
            pltpu.VMEM((SPAN_J, FRAMES, 512), BF16),
            pltpu.VMEM((SPAN_I, PAIRS, FRAMES, 128), BF16),
            pltpu.VMEM((SPAN_I, FRAMES, HALF), F32),
            pltpu.VMEM((SPAN_I, FRAMES, HALF), F32),
            pltpu.VMEM((SPAN_I, FRAMES, HALF), F32),
            pltpu.VMEM((SPAN_I - 1, FRAMES, HALF), BF16),
            pltpu.VMEM((SPAN_I - 1, FRAMES, HALF), BF16),
            dma, dma, dma, dma((PIX_CHUNKS,)), dma((R_CHUNKS,)), dma((SPAN_I,)),
            dma, dma, dma, dma,
            dma((SPAN_I,)), dma((SPAN_I,)),
            dma((SPAN_I - 1,)), dma((SPAN_I - 1,)),
        ],
        compiler_params=pltpu.CompilerParams(
            collective_id=0, has_side_effects=True, vmem_limit_bytes=64 * 1024 * 1024 - 65536
        ),
        name="frames_to_commands",
    )(
        column_order.reshape(1, -1),
        tile_ranks,
        jnp.transpose(pixels, (0, 2, 1)),
        jnp.transpose(match_filter, (1, 2, 0)),
        right_factors,
        left_factors,
    )


def solution(mesh):
    in_specs = (
        P(None, ("row", "col"), None),
        P(("row", "col"), None, None),
        P("row", "col"),
        P(),
        P("row", "col", None, None),
        P("row", "col", None, None),
    )
    out_specs = P(None, ("row", "col"))
    return jax.shard_map(shards, mesh=mesh, in_specs=in_specs, out_specs=out_specs, check_vma=False)
```

```python
import jax
import jax.numpy as jnp
from jax import lax
from jax.experimental import pallas as pl
from jax.experimental.pallas import tpu as pltpu
from jax.sharding import PartitionSpec as P

BF16 = jnp.bfloat16
F32 = jnp.float32
ROWS, COLS = 8, 16
FRAMES, SUBS, PIX = 64, 500, 144
TILE, RANK = 500, 64
SPAN_I, SPAN_J = 8, 16
HALF = 250
PIX_CHUNKS = 8
CHUNK_FRAMES = FRAMES // PIX_CHUNKS
R_CHUNKS = 4
R_COLS = SPAN_J // R_CHUNKS
PAIRS = SPAN_J // 2
CHUNK_PAIRS = PAIRS // R_CHUNKS
DEVICES = ROWS * COLS
MESH = pl.DeviceIdType.MESH


def one_hot(shape, target_of_row):
    row = lax.broadcasted_iota(jnp.int32, shape, 0)
    col = lax.broadcasted_iota(jnp.int32, shape, 1)
    return jnp.where(col == target_of_row(row), 1.0, 0.0).astype(BF16)


def permute(matrix, rows):
    return jnp.dot(matrix, rows, preferred_element_type=F32).astype(BF16)


def kernel(
    order_hbm, ranks_hbm, pix_hbm, filt_hbm, right_hbm, left_hbm, out_ref,
    order, ranks, pix, filt, filt32, right, left, slopes, sel, lanes, frame_rows, rows32, folds, by_piece, at_mid, by_col, gathered,
    pieces, proj, other_half, my_half, half_in, chunk_out, chunk_in,
    order_sem, ranks_sem, filt_sem, pix_sem, right_sem, left_sem,
    spread_send, spread_recv, gather_send, gather_recv,
    c1_send, c1_recv, c2_send, c2_recv,
):
    r = lax.axis_index("row")
    c = lax.axis_index("col")
    core = lax.rem(c, 2)
    y = lax.rem(c // 2, 4)
    z_hi = c // 8
    x = r // 2
    z = z_hi * 2 + lax.rem(r, 2)
    rank = r * COLS + c

    xs = [lax.rem(x + d, 4) for d in range(4)]
    ys = [lax.rem(y + d, 4) for d in range(4)]
    zs = [lax.rem(z + d, 4) for d in range(4)]
    cores = [core, 1 - core]
    offsets = [(dx, dy, dz, dk) for dx in range(4) for dy in range(4) for dz in range(4) for dk in range(2)]
    offsets.sort(key=lambda o: -sum(min(d, 4 - d) for d in o[:3]))
    peers = [
        (xs[dx] * 2 + lax.rem(zs[dz], 2), (zs[dz] // 2 * 4 + ys[dy]) * 2 + cores[dk])
        for dx, dy, dz, dk in offsets
        if (dx, dy, dz, dk) != (0, 0, 0, 0)
    ]

    def pix_copy(n):
        frames = pl.ds(n * CHUNK_FRAMES, CHUNK_FRAMES)
        return pltpu.make_async_copy(pix_hbm.at[frames], pix.at[frames], pix_sem.at[n])

    def right_copy(n):
        cols = pl.ds(n * R_COLS, R_COLS)
        return pltpu.make_async_copy(right_hbm.at[:, cols], right.at[:, cols], right_sem.at[n])

    def left_copy(n):
        return pltpu.make_async_copy(left_hbm.at[n], left.at[n], left_sem.at[n])

    order_copy = pltpu.make_async_copy(order_hbm, order, order_sem)
    ranks_copy = pltpu.make_async_copy(ranks_hbm, ranks, ranks_sem)
    filt_copy = pltpu.make_async_copy(filt_hbm, filt, filt_sem)
    filt_copy.start()
    order_copy.start()
    ranks_copy.start()
    for n in range(PIX_CHUNKS):
        pix_copy(n).start()
    barrier = pltpu.get_barrier_semaphore()
    for row, col in peers:
        pl.semaphore_signal(barrier, inc=1, device_id={"row": row, "col": col}, device_id_type=MESH)

    order_copy.wait()
    wanted = jnp.broadcast_to(order[...].astype(F32), (128, 256)).T
    source = lax.broadcasted_iota(jnp.int32, (256, 128), 1)
    for b in range(2):
        match = (source * 2 + b).astype(F32) == wanted
        sel[:, b * 128 : b * 128 + 128] = jnp.where(match, 1.0, 0.0).astype(BF16)
    lanes[...] = one_hot((256, 256), lambda row: (row & 127) * 2 + (row >> 7))
    frame_rows[...] = one_hot((256, 256), lambda row: (row & 31) * 8 + (row >> 5))
    rows32[...] = jnp.zeros_like(rows32)
    slopes[...] = jnp.zeros_like(slopes)
    folds[...] = jnp.zeros_like(folds)

    filt_copy.wait()
    filt32[...] = filt[...].astype(F32)

    def centroid(n, carry):
        pix_copy(n).wait()
        for lane in range(4):
            low, high = lane * 128, min(lane * 128 + 128, SUBS)
            width = high - low

            zero = jnp.zeros((8, width), F32)
            sums = [[zero] * CHUNK_FRAMES for _ in range(3)]
            for p in range(0, PIX, 16):
                fx = filt32[0, p : p + 16, low:high]
                fy = filt32[1, p : p + 16, low:high]
                for f in range(CHUNK_FRAMES):
                    v = pix[n * CHUNK_FRAMES + f, p : p + 16, low:high].astype(F32)
                    vx, vy = v * fx, v * fy
                    sums[0][f] = sums[0][f] + (v[:8] + v[8:])
                    sums[1][f] = sums[1][f] + (vx[:8] + vx[8:])
                    sums[2][f] = sums[2][f] + (vy[:8] + vy[8:])
            for kind in range(3):
                for f in range(CHUNK_FRAMES):
                    first = (lane * 3 + kind) * 64 + f * 8
                    folds[first : first + 8, :width] = sums[kind][f]

            def total(kind):
                first = (lane * 3 + kind) * 64
                return sum(folds[pl.ds(first + k, CHUNK_FRAMES, stride=8), :] for k in range(8))[:, :width]

            flux = total(0)
            frames = pl.ds(pl.multiple_of(n * CHUNK_FRAMES, 8), CHUNK_FRAMES)
            slopes[0, frames, low:high] = total(1) / flux
            slopes[1, frames, low:high] = total(2) / flux
        return carry

    lax.fori_loop(0, PIX_CHUNKS, centroid, 0)

    parts = []
    for b in range(2):
        kinds = [slopes[k] if b == 0 else pltpu.roll(slopes[k], 512 - HALF, 1) for k in range(2)]
        for h in range(2):
            parts.append(jnp.concatenate([v[:, h * 128 : h * 128 + 128] for v in kinds], axis=1))
    raw = jnp.concatenate(parts, axis=0).astype(BF16)
    raw = jnp.dot(raw, lanes[...], preferred_element_type=F32)

    for b in range(2):
        for h in range(2):
            for q in range(2):
                first = b * 128 + h * 64
                rows32[pl.ds(h * 8 + b * 2 + q, FRAMES, stride=16), :] = raw[
                    first : first + FRAMES, q * 128 : q * 128 + 128
                ]
    by_piece[...] = rows32[...].reshape(DEVICES, 8, 128).astype(BF16)

    pl.semaphore_wait(barrier, DEVICES - 1)

    def remote(src, dst, send, recv, device):
        return pltpu.make_async_remote_copy(
            src_ref=src, dst_ref=dst, send_sem=send, recv_sem=recv, device_id=device, device_id_type=MESH
        )

    for row, col in peers:
        remote(
            by_piece.at[row * COLS + col], at_mid.at[rank], spread_send, spread_recv, {"row": row, "col": col}
        ).start()
    at_mid[rank] = by_piece[rank]
    for n in range(R_CHUNKS):
        right_copy(n).start()
    others = pl.ds(0, DEVICES - 1)
    spread = remote(by_piece.at[others], at_mid.at[others], spread_send, spread_recv, {"row": r})
    spread.wait_recv()
    rows32[...] = at_mid[...].astype(F32).reshape(DEVICES * 8, 128)
    every = jnp.concatenate(
        [
            jnp.concatenate([rows32[pl.ds(b * 2 + q, DEVICES, stride=8), :] for q in range(2)], axis=1)
            for b in range(2)
        ],
        axis=0,
    ).astype(BF16)
    chosen = jnp.dot(sel[...], every, preferred_element_type=F32).reshape(COLS, 2, SPAN_J // 2, 256)
    for part in range(2):
        by_col[part] = chosen[:, part].astype(BF16)

    for part in range(2):
        for row, col in peers:
            remote(
                by_col.at[part, col], gathered.at[part, rank], gather_send.at[part], gather_recv.at[part],
                {"row": row, "col": col},
            ).start()
        gathered[part, rank] = by_col[part, c]
    gather = [
        remote(
            gathered.at[part, others], gathered.at[part, others], gather_send.at[part], gather_recv.at[part],
            {"row": r},
        )
        for part in range(2)
    ]
    for n in range(SPAN_I):
        left_copy(n).start()
    ranks_copy.wait()

    def arrive(part):
        right_copy(2 * part).wait()
        right_copy(2 * part + 1).wait()
        gather[part].wait_recv()
        for g in range(2):
            for h in range(2):
                rows = jnp.concatenate(
                    [gathered[part, 2 * (g * 32 + f) + h].astype(F32) for f in range(32)], axis=0
                ).astype(BF16)
                pieces[part * 8 : part * 8 + 8, g * 32 : g * 32 + 32, h * 256 : h * 256 + 256] = permute(
                    frame_rows[...], rows
                ).reshape(SPAN_J // 2, 32, 256)

    lane_id = lax.broadcasted_iota(jnp.int32, (FRAMES, 128), 1)
    low_half = lane_id < RANK
    component = lane_id & (RANK - 1)

    def project(n, first):
        for q in range(CHUNK_PAIRS):
            pair = n * CHUNK_PAIRS + q
            halves = []
            for e in range(2):
                factors = right[pl.ds(first, 4), 2 * pair + e].reshape(4 * RANK, TILE)
                halves.append(
                    lax.dot_general(
                        pieces[2 * pair + e][:, :TILE], factors, (((1,), (1,)), ((), ())), preferred_element_type=F32
                    )
                )
            for i2 in range(2):
                i = first + 2 * i2
                kept = []
                for e in range(2):
                    bound = jnp.where(low_half, ranks[i, 2 * pair + e], ranks[i + 1, 2 * pair + e])
                    kept.append(jnp.where(component < bound, halves[e][:, i2 * 128 : i2 * 128 + 128], 0.0))
                proj[i, pair] = jnp.where(low_half, kept[0], pltpu.roll(kept[1], RANK, 1)).astype(BF16)
                proj[i + 1, pair] = jnp.where(low_half, pltpu.roll(kept[0], RANK, 1), kept[1]).astype(BF16)

    def project_early(n, carry):
        project(lax.rem(n, 2), n // 2 * 4)
        return carry

    far, near = (1 - z_hi) * 4, z_hi * 4
    arrive(0)
    lax.fori_loop(0, 4, project_early, 0)
    arrive(1)

    def half_copy(s):
        return remote(
            other_half.at[s], half_in.at[s], c1_send.at[s], c1_recv.at[s], {"row": r, "col": c + 1 - 2 * core}
        )

    def tile_of(s):
        return lax.rem(z_hi + 1 - s // 4, 2) * 4 + lax.rem(y + 1 + s, 4)

    def chunk_copy(s):
        return remote(
            chunk_out.at[s], chunk_in.at[s], c2_send.at[s], c2_recv.at[s], {"row": r, "col": 2 * tile_of(s) + core}
        )

    def finish(s):
        half_copy(s).wait_recv()
        chunk_out[s] = (my_half[s] + half_in[s]).astype(BF16)
        chunk_copy(s).start()

    def command(s, carry):
        i = tile_of(s)
        lhs = jnp.concatenate([proj[i, q] for q in range(PAIRS)], axis=1)
        full = jnp.dot(lhs, left[i].reshape(SPAN_J * RANK, TILE), preferred_element_type=F32)
        lower, upper = full[:, :HALF], full[:, HALF:]
        first = core == 0
        my_half[s] = jnp.where(first, lower, upper)
        other_half[s] = jnp.where(first, upper, lower)
        half_copy(s).start()

        @pl.when(lax.rem(s, 4) > 0)
        def _():
            finish(s - 1)

        return carry

    project(2, far)
    project(3, far)
    for n in range(SPAN_I):
        left_copy(n).wait()
    lax.fori_loop(0, 4, command, 0)
    project(2, near)
    finish(3)
    project(3, near)
    lax.fori_loop(4, SPAN_I, command, 0)
    last = SPAN_I - 1
    half_copy(last).wait_recv()
    total_cmd = my_half[last] + half_in[last]
    for s in range(last):
        chunk_copy(s).wait_recv()
        total_cmd += chunk_in[s].astype(F32)
    out_ref[...] = total_cmd

    spread.wait_send()
    for part in range(2):
        gather[part].wait_send()
    for s in range(SPAN_I):
        half_copy(s).wait_send()
    for s in range(last):
        chunk_copy(s).wait_send()


def shards(pixels, match_filter, tile_ranks, column_order, right_factors, left_factors):
    hbm = pl.BlockSpec(memory_space=pltpu.HBM)
    dma = pltpu.SemaphoreType.DMA
    return pl.pallas_call(
        kernel,
        out_shape=jax.ShapeDtypeStruct((FRAMES, HALF), F32),
        in_specs=[hbm] * 6,
        out_specs=pl.BlockSpec(memory_space=pltpu.VMEM),
        scratch_shapes=[
            pltpu.VMEM((1, 256), jnp.int32),
            pltpu.SMEM((SPAN_I, SPAN_J), jnp.int32),
            pltpu.VMEM((FRAMES, PIX, SUBS), BF16),
            pltpu.VMEM((2, PIX, SUBS), BF16),
            pltpu.VMEM((2, PIX, SUBS), F32),
            pltpu.VMEM((SPAN_I, SPAN_J, RANK, TILE), BF16),
            pltpu.VMEM((SPAN_I, SPAN_J, RANK, TILE), BF16),
            pltpu.VMEM((2, FRAMES, 512), F32),
            pltpu.VMEM((256, 256), BF16),
            pltpu.VMEM((256, 256), BF16),
            pltpu.VMEM((256, 256), BF16),
            pltpu.VMEM((DEVICES * 8, 128), F32),
            pltpu.VMEM((4 * 3 * 64, 128), F32),
            pltpu.VMEM((DEVICES, 8, 128), BF16),
            pltpu.VMEM((DEVICES, 8, 128), BF16),
            pltpu.VMEM((2, COLS, SPAN_J // 2, 256), BF16),
            pltpu.VMEM((2, DEVICES, SPAN_J // 2, 256), BF16),
            pltpu.VMEM((SPAN_J, FRAMES, 512), BF16),
            pltpu.VMEM((SPAN_I, PAIRS, FRAMES, 128), BF16),
            pltpu.VMEM((SPAN_I, FRAMES, HALF), F32),
            pltpu.VMEM((SPAN_I, FRAMES, HALF), F32),
            pltpu.VMEM((SPAN_I, FRAMES, HALF), F32),
            pltpu.VMEM((SPAN_I - 1, FRAMES, HALF), BF16),
            pltpu.VMEM((SPAN_I - 1, FRAMES, HALF), BF16),
            dma, dma, dma, dma((PIX_CHUNKS,)), dma((R_CHUNKS,)), dma((SPAN_I,)),
            dma, dma, dma((2,)), dma((2,)),
            dma((SPAN_I,)), dma((SPAN_I,)),
            dma((SPAN_I - 1,)), dma((SPAN_I - 1,)),
        ],
        compiler_params=pltpu.CompilerParams(
            collective_id=0, has_side_effects=True, vmem_limit_bytes=64 * 1024 * 1024 - 65536
        ),
        name="frames_to_commands",
    )(
        column_order.reshape(1, -1),
        tile_ranks,
        jnp.transpose(pixels, (0, 2, 1)),
        jnp.transpose(match_filter, (1, 2, 0)),
        right_factors,
        left_factors,
    )


def solution(mesh):
    in_specs = (
        P(None, ("row", "col"), None),
        P(("row", "col"), None, None),
        P("row", "col"),
        P(),
        P("row", "col", None, None),
        P("row", "col", None, None),
    )
    out_specs = P(None, ("row", "col"))
    return jax.shard_map(shards, mesh=mesh, in_specs=in_specs, out_specs=out_specs, check_vma=False)
```

```python
import jax
import jax.numpy as jnp
from jax import lax
from jax.experimental import pallas as pl
from jax.experimental.pallas import tpu as pltpu
from jax.sharding import PartitionSpec as P

BF16 = jnp.bfloat16
F32 = jnp.float32
ROWS, COLS = 8, 16
FRAMES, SUBS, PIX = 64, 500, 144
TILE, RANK = 500, 64
SPAN_I, SPAN_J = 8, 16
HALF = 250
PIX_CHUNKS = 8
CHUNK_FRAMES = FRAMES // PIX_CHUNKS
R_CHUNKS = 4
R_COLS = SPAN_J // R_CHUNKS
PAIRS = SPAN_J // 2
CHUNK_PAIRS = PAIRS // R_CHUNKS
DEVICES = ROWS * COLS
MESH = pl.DeviceIdType.MESH


def one_hot(shape, target_of_row):
    row = lax.broadcasted_iota(jnp.int32, shape, 0)
    col = lax.broadcasted_iota(jnp.int32, shape, 1)
    return jnp.where(col == target_of_row(row), 1.0, 0.0).astype(BF16)


def permute(matrix, rows):
    return jnp.dot(matrix, rows, preferred_element_type=F32).astype(BF16)


def kernel(
    order_hbm, ranks_hbm, pix_hbm, filt_hbm, right_hbm, left_hbm, out_ref,
    order, ranks, pix, filt, filt32, right, left, slopes, sel, lanes, frame_rows, rows32, folds, by_piece, at_mid, by_col, gathered,
    pieces, proj, other_half, my_half, half_in, chunk_out, chunk_in,
    order_sem, ranks_sem, filt_sem, pix_sem, right_sem, left_sem,
    spread_send, spread_recv, gather_send, gather_recv,
    c1_send, c1_recv, c2_send, c2_recv,
):
    r = lax.axis_index("row")
    c = lax.axis_index("col")
    core = lax.rem(c, 2)
    y = lax.rem(c // 2, 4)
    z_hi = c // 8
    x = r // 2
    z = z_hi * 2 + lax.rem(r, 2)
    rank = r * COLS + c

    xs = [lax.rem(x + d, 4) for d in range(4)]
    ys = [lax.rem(y + d, 4) for d in range(4)]
    zs = [lax.rem(z + d, 4) for d in range(4)]
    cores = [core, 1 - core]
    offsets = [(dx, dy, dz, dk) for dx in range(4) for dy in range(4) for dz in range(4) for dk in range(2)]
    offsets.sort(key=lambda o: -sum(min(d, 4 - d) for d in o[:3]))
    peers_at = {d: [] for d in range(4)}
    peers = []
    for dx, dy, dz, dk in offsets:
        if (dx, dy, dz, dk) != (0, 0, 0, 0):
            peer = (xs[dx] * 2 + lax.rem(zs[dz], 2), (zs[dz] // 2 * 4 + ys[dy]) * 2 + cores[dk])
            peers.append(peer)
            peers_at[dx].append(peer)

    def pix_copy(n):
        frames = pl.ds(n * CHUNK_FRAMES, CHUNK_FRAMES)
        return pltpu.make_async_copy(pix_hbm.at[frames], pix.at[frames], pix_sem.at[n])

    def right_copy(n):
        cols = pl.ds(n * R_COLS, R_COLS)
        return pltpu.make_async_copy(right_hbm.at[:, cols], right.at[:, cols], right_sem.at[n])

    def left_copy(n):
        return pltpu.make_async_copy(left_hbm.at[n], left.at[n], left_sem.at[n])

    order_copy = pltpu.make_async_copy(order_hbm, order, order_sem)
    ranks_copy = pltpu.make_async_copy(ranks_hbm, ranks, ranks_sem)
    filt_copy = pltpu.make_async_copy(filt_hbm, filt, filt_sem)
    filt_copy.start()
    order_copy.start()
    ranks_copy.start()
    for n in range(PIX_CHUNKS):
        pix_copy(n).start()
    barrier = pltpu.get_barrier_semaphore()
    for row, col in peers:
        pl.semaphore_signal(barrier, inc=1, device_id={"row": row, "col": col}, device_id_type=MESH)

    order_copy.wait()
    wanted = jnp.broadcast_to(order[...].astype(F32), (128, 256)).T
    source = lax.broadcasted_iota(jnp.int32, (256, 128), 1)
    for b in range(2):
        match = (source * 2 + b).astype(F32) == wanted
        sel[:, b * 128 : b * 128 + 128] = jnp.where(match, 1.0, 0.0).astype(BF16)
    lanes[...] = one_hot((256, 256), lambda row: (row & 127) * 2 + (row >> 7))
    frame_rows[...] = one_hot((256, 256), lambda row: (row & 31) * 8 + (row >> 5))
    rows32[...] = jnp.zeros_like(rows32)
    slopes[...] = jnp.zeros_like(slopes)
    folds[...] = jnp.zeros_like(folds)

    filt_copy.wait()
    filt32[...] = filt[...].astype(F32)

    def centroid(n, carry):
        pix_copy(n).wait()
        for lane in range(4):
            low, high = lane * 128, min(lane * 128 + 128, SUBS)
            width = high - low

            zero = jnp.zeros((8, width), F32)
            sums = [[zero] * CHUNK_FRAMES for _ in range(3)]
            for p in range(0, PIX, 16):
                fx = filt32[0, p : p + 16, low:high]
                fy = filt32[1, p : p + 16, low:high]
                for f in range(CHUNK_FRAMES):
                    v = pix[n * CHUNK_FRAMES + f, p : p + 16, low:high].astype(F32)
                    vx, vy = v * fx, v * fy
                    sums[0][f] = sums[0][f] + (v[:8] + v[8:])
                    sums[1][f] = sums[1][f] + (vx[:8] + vx[8:])
                    sums[2][f] = sums[2][f] + (vy[:8] + vy[8:])
            for kind in range(3):
                for f in range(CHUNK_FRAMES):
                    first = (lane * 3 + kind) * 64 + f * 8
                    folds[first : first + 8, :width] = sums[kind][f]

            def total(kind):
                first = (lane * 3 + kind) * 64
                return sum(folds[pl.ds(first + k, CHUNK_FRAMES, stride=8), :] for k in range(8))[:, :width]

            flux = total(0)
            frames = pl.ds(pl.multiple_of(n * CHUNK_FRAMES, 8), CHUNK_FRAMES)
            slopes[0, frames, low:high] = total(1) / flux
            slopes[1, frames, low:high] = total(2) / flux
        return carry

    lax.fori_loop(0, PIX_CHUNKS, centroid, 0)

    parts = []
    for b in range(2):
        kinds = [slopes[k] if b == 0 else pltpu.roll(slopes[k], 512 - HALF, 1) for k in range(2)]
        for h in range(2):
            parts.append(jnp.concatenate([v[:, h * 128 : h * 128 + 128] for v in kinds], axis=1))
    raw = jnp.concatenate(parts, axis=0).astype(BF16)
    raw = jnp.dot(raw, lanes[...], preferred_element_type=F32)

    for b in range(2):
        for h in range(2):
            for q in range(2):
                first = b * 128 + h * 64
                rows32[pl.ds(h * 8 + b * 2 + q, FRAMES, stride=16), :] = raw[
                    first : first + FRAMES, q * 128 : q * 128 + 128
                ]
    by_piece[...] = rows32[...].reshape(DEVICES, 8, 128).astype(BF16)

    pl.semaphore_wait(barrier, DEVICES - 1)

    def remote(src, dst, send, recv, device):
        return pltpu.make_async_remote_copy(
            src_ref=src, dst_ref=dst, send_sem=send, recv_sem=recv, device_id=device, device_id_type=MESH
        )

    for row, col in peers:
        remote(
            by_piece.at[row * COLS + col, pl.ds(0, 4)], at_mid.at[rank, pl.ds(0, 4)], spread_send, spread_recv, {"row": row, "col": col}
        ).start()
    at_mid[rank] = by_piece[rank]
    for n in range(R_CHUNKS):
        right_copy(n).start()
    others = pl.ds(0, DEVICES - 1)
    spread = remote(by_piece.at[others, pl.ds(0, 4)], at_mid.at[others, pl.ds(0, 4)], spread_send, spread_recv, {"row": r})
    spread.wait_recv()
    rows32[...] = at_mid[...].astype(F32).reshape(DEVICES * 8, 128)
    every = jnp.concatenate(
        [
            jnp.concatenate([rows32[pl.ds(b * 2 + q, DEVICES, stride=8), :] for q in range(2)], axis=1)
            for b in range(2)
        ],
        axis=0,
    ).astype(BF16)
    chosen = jnp.dot(sel[...], every, preferred_element_type=F32).reshape(COLS, 2, SPAN_J // 2, 256)
    for part in range(2):
        by_col[part] = chosen[:, part].astype(BF16)

    def gather_to(part, dx):
        for row, col in peers_at[dx]:
            remote(
                by_col.at[part, col], gathered.at[part, rank], gather_send.at[part, dx], gather_recv.at[part, dx],
                {"row": row, "col": col},
            ).start()

    def gathered_at(part, dx):
        slots = pl.ds(0, len(peers_at[dx]))
        return remote(
            gathered.at[part, slots], gathered.at[part, slots], gather_send.at[part, dx], gather_recv.at[part, dx],
            {"row": r},
        )

    def relay(part):
        slots = pl.ds(xs[3 if part == 0 else 1] * 32, 32)
        return remote(
            gathered.at[part, slots], gathered.at[part, slots], gather_send.at[part, 2], gather_recv.at[part, 2],
            {"row": xs[1 if part == 0 else 3] * 2 + lax.rem(r, 2), "col": c},
        )

    gather_to(0, 1)
    gather_to(1, 3)
    gather_to(0, 3)
    gather_to(0, 0)
    gathered[0, rank] = by_col[0, c]
    gathered_at(0, 1).wait_recv()
    relay(0).start()
    gather_to(1, 1)
    gathered_at(1, 3).wait_recv()
    relay(1).start()
    gather_to(1, 0)
    gathered[1, rank] = by_col[1, c]
    for n in range(SPAN_I):
        left_copy(n).start()
    ranks_copy.wait()

    def arrive(part):
        right_copy(2 * part).wait()
        right_copy(2 * part + 1).wait()
        gathered_at(part, 3 if part == 0 else 1).wait_recv()
        gathered_at(part, 0).wait_recv()
        relay(part).wait_recv()
        for g in range(2):
            for h in range(2):
                rows = jnp.concatenate(
                    [gathered[part, 2 * (g * 32 + f) + h].astype(F32) for f in range(32)], axis=0
                ).astype(BF16)
                pieces[part * 8 : part * 8 + 8, g * 32 : g * 32 + 32, h * 256 : h * 256 + 256] = permute(
                    frame_rows[...], rows
                ).reshape(SPAN_J // 2, 32, 256)

    lane_id = lax.broadcasted_iota(jnp.int32, (FRAMES, 128), 1)
    low_half = lane_id < RANK
    component = lane_id & (RANK - 1)

    def project(n, first):
        for q in range(CHUNK_PAIRS):
            pair = n * CHUNK_PAIRS + q
            halves = []
            for e in range(2):
                factors = right[pl.ds(first, 4), 2 * pair + e].reshape(4 * RANK, TILE)
                halves.append(
                    lax.dot_general(
                        pieces[2 * pair + e][:, :TILE], factors, (((1,), (1,)), ((), ())), preferred_element_type=F32
                    )
                )
            for i2 in range(2):
                i = first + 2 * i2
                kept = []
                for e in range(2):
                    bound = jnp.where(low_half, ranks[i, 2 * pair + e], ranks[i + 1, 2 * pair + e])
                    kept.append(jnp.where(component < bound, halves[e][:, i2 * 128 : i2 * 128 + 128], 0.0))
                proj[i, pair] = jnp.where(low_half, kept[0], pltpu.roll(kept[1], RANK, 1)).astype(BF16)
                proj[i + 1, pair] = jnp.where(low_half, pltpu.roll(kept[0], RANK, 1), kept[1]).astype(BF16)

    def project_early(n, carry):
        project(lax.rem(n, 2), n // 2 * 4)
        return carry

    far, near = (1 - z_hi) * 4, z_hi * 4
    arrive(0)
    lax.fori_loop(0, 4, project_early, 0)
    arrive(1)

    def half_copy(s):
        return remote(
            other_half.at[s], half_in.at[s], c1_send.at[s], c1_recv.at[s], {"row": r, "col": c + 1 - 2 * core}
        )

    def tile_of(s):
        return lax.rem(z_hi + 1 - s // 4, 2) * 4 + lax.rem(y + 1 + s, 4)

    def chunk_copy(s):
        return remote(
            chunk_out.at[s], chunk_in.at[s], c2_send.at[s], c2_recv.at[s], {"row": r, "col": 2 * tile_of(s) + core}
        )

    def finish(s):
        half_copy(s).wait_recv()
        chunk_out[s] = (my_half[s] + half_in[s]).astype(BF16)
        chunk_copy(s).start()

    def commands(steps):
        full = []
        for s in steps:
            i = tile_of(s)
            lhs = jnp.concatenate([proj[i, q] for q in range(PAIRS)], axis=1)
            full.append(jnp.dot(lhs, left[i].reshape(SPAN_J * RANK, TILE), preferred_element_type=F32))
        first = core == 0
        for s, tile in zip(steps, full):
            lower, upper = tile[:, :HALF], tile[:, HALF:]
            other_half[s] = jnp.where(first, upper, lower)
            my_half[s] = jnp.where(first, lower, upper)
            half_copy(s).start()

    project(2, far)
    project(3, far)
    for n in range(SPAN_I):
        left_copy(n).wait()
    commands((0, 1))
    commands((2, 3))
    finish(0)
    finish(1)
    project(2, near)
    finish(2)
    finish(3)
    project(3, near)
    commands((4, 5))
    commands((6, 7))
    for s in range(4, 7):
        finish(s)
    last = SPAN_I - 1
    half_copy(last).wait_recv()
    total_cmd = my_half[last] + half_in[last]
    for s in range(last):
        chunk_copy(s).wait_recv()
        total_cmd += chunk_in[s].astype(F32)
    out_ref[...] = total_cmd

    spread.wait_send()
    for part in range(2):
        for dx in (0, 1, 3):
            gathered_at(part, dx).wait_send()
        relay(part).wait_send()
    for s in range(SPAN_I):
        half_copy(s).wait_send()
    for s in range(last):
        chunk_copy(s).wait_send()


def shards(pixels, match_filter, tile_ranks, column_order, right_factors, left_factors):
    hbm = pl.BlockSpec(memory_space=pltpu.HBM)
    dma = pltpu.SemaphoreType.DMA
    return pl.pallas_call(
        kernel,
        out_shape=jax.ShapeDtypeStruct((FRAMES, HALF), F32),
        in_specs=[hbm] * 6,
        out_specs=pl.BlockSpec(memory_space=pltpu.VMEM),
        scratch_shapes=[
            pltpu.VMEM((1, 256), jnp.int32),
            pltpu.SMEM((SPAN_I, SPAN_J), jnp.int32),
            pltpu.VMEM((FRAMES, PIX, SUBS), BF16),
            pltpu.VMEM((2, PIX, SUBS), BF16),
            pltpu.VMEM((2, PIX, SUBS), F32),
            pltpu.VMEM((SPAN_I, SPAN_J, RANK, TILE), BF16),
            pltpu.VMEM((SPAN_I, SPAN_J, RANK, TILE), BF16),
            pltpu.VMEM((2, FRAMES, 512), F32),
            pltpu.VMEM((256, 256), BF16),
            pltpu.VMEM((256, 256), BF16),
            pltpu.VMEM((256, 256), BF16),
            pltpu.VMEM((DEVICES * 8, 128), F32),
            pltpu.VMEM((4 * 3 * 64, 128), F32),
            pltpu.VMEM((DEVICES, 8, 128), BF16),
            pltpu.VMEM((DEVICES, 8, 128), BF16),
            pltpu.VMEM((2, COLS, SPAN_J // 2, 256), BF16),
            pltpu.VMEM((2, DEVICES, SPAN_J // 2, 256), BF16),
            pltpu.VMEM((SPAN_J, FRAMES, 512), BF16),
            pltpu.VMEM((SPAN_I, PAIRS, FRAMES, 128), BF16),
            pltpu.VMEM((SPAN_I, FRAMES, HALF), F32),
            pltpu.VMEM((SPAN_I, FRAMES, HALF), F32),
            pltpu.VMEM((SPAN_I, FRAMES, HALF), F32),
            pltpu.VMEM((SPAN_I - 1, FRAMES, HALF), BF16),
            pltpu.VMEM((SPAN_I - 1, FRAMES, HALF), BF16),
            dma, dma, dma, dma((PIX_CHUNKS,)), dma((R_CHUNKS,)), dma((SPAN_I,)),
            dma, dma, dma((2, 4)), dma((2, 4)),
            dma((SPAN_I,)), dma((SPAN_I,)),
            dma((SPAN_I - 1,)), dma((SPAN_I - 1,)),
        ],
        compiler_params=pltpu.CompilerParams(
            collective_id=0, has_side_effects=True, vmem_limit_bytes=64 * 1024 * 1024 - 65536
        ),
        name="frames_to_commands",
    )(
        column_order.reshape(1, -1),
        tile_ranks,
        jnp.transpose(pixels, (0, 2, 1)),
        jnp.transpose(match_filter, (1, 2, 0)),
        right_factors,
        left_factors,
    )


def solution(mesh):
    in_specs = (
        P(None, ("row", "col"), None),
        P(("row", "col"), None, None),
        P("row", "col"),
        P(),
        P("row", "col", None, None),
        P("row", "col", None, None),
    )
    out_specs = P(None, ("row", "col"))
    return jax.shard_map(shards, mesh=mesh, in_specs=in_specs, out_specs=out_specs, check_vma=False)
```

```python
import jax
import jax.numpy as jnp
from jax import lax
from jax.experimental import pallas as pl
from jax.experimental.pallas import tpu as pltpu
from jax.sharding import PartitionSpec as P

BF16 = jnp.bfloat16
F32 = jnp.float32
ROWS, COLS = 8, 16
FRAMES, SUBS, PIX = 64, 500, 144
TILE, RANK = 500, 64
SPAN_I, SPAN_J = 8, 16
HALF = 250
PIX_CHUNKS = 8
CHUNK_FRAMES = FRAMES // PIX_CHUNKS
R_CHUNKS = 4
R_COLS = SPAN_J // R_CHUNKS
PAIRS = SPAN_J // 2
CHUNK_PAIRS = PAIRS // R_CHUNKS
DEVICES = ROWS * COLS
MESH = pl.DeviceIdType.MESH


def one_hot(shape, target_of_row):
    row = lax.broadcasted_iota(jnp.int32, shape, 0)
    col = lax.broadcasted_iota(jnp.int32, shape, 1)
    return jnp.where(col == target_of_row(row), 1.0, 0.0).astype(BF16)


def permute(matrix, rows):
    return jnp.dot(matrix, rows, preferred_element_type=F32).astype(BF16)


def kernel(
    order_hbm, ranks_hbm, pix_hbm, filt_hbm, right_hbm, left_hbm, out_ref,
    order, ranks, pix, filt, filt32, right, left, slopes, sel, lanes, frame_rows, rows32, folds, by_piece, at_mid, by_col, gathered,
    pieces, proj, other_half, my_half, early, half_in, chunk_out, chunk_in, direct_out, direct_in,
    order_sem, ranks_sem, filt_sem, pix_sem, right_sem, left_sem,
    spread_send, spread_recv, gather_send, gather_recv,
    c1_send, c1_recv, c2_send, c2_recv, direct_send, direct_recv,
):
    r = lax.axis_index("row")
    c = lax.axis_index("col")
    core = lax.rem(c, 2)
    y = lax.rem(c // 2, 4)
    z_hi = c // 8
    x = r // 2
    z = z_hi * 2 + lax.rem(r, 2)
    rank = r * COLS + c

    xs = [lax.rem(x + d, 4) for d in range(4)]
    ys = [lax.rem(y + d, 4) for d in range(4)]
    zs = [lax.rem(z + d, 4) for d in range(4)]
    cores = [core, 1 - core]
    offsets = [(dx, dy, dz, dk) for dx in range(4) for dy in range(4) for dz in range(4) for dk in range(2)]
    offsets.sort(key=lambda o: -sum(min(d, 4 - d) for d in o[:3]))
    peers_at = {d: [] for d in range(4)}
    peers = []
    for dx, dy, dz, dk in offsets:
        if (dx, dy, dz, dk) != (0, 0, 0, 0):
            peer = (xs[dx] * 2 + lax.rem(zs[dz], 2), (zs[dz] // 2 * 4 + ys[dy]) * 2 + cores[dk])
            peers.append(peer)
            peers_at[dx].append(peer)

    def pix_copy(n):
        frames = pl.ds(n * CHUNK_FRAMES, CHUNK_FRAMES)
        return pltpu.make_async_copy(pix_hbm.at[frames], pix.at[frames], pix_sem.at[n])

    def right_copy(n):
        cols = pl.ds(n * R_COLS, R_COLS)
        return pltpu.make_async_copy(right_hbm.at[:, cols], right.at[:, cols], right_sem.at[n])

    def left_copy(n):
        return pltpu.make_async_copy(left_hbm.at[n], left.at[n], left_sem.at[n])

    order_copy = pltpu.make_async_copy(order_hbm, order, order_sem)
    ranks_copy = pltpu.make_async_copy(ranks_hbm, ranks, ranks_sem)
    filt_copy = pltpu.make_async_copy(filt_hbm, filt, filt_sem)
    filt_copy.start()
    order_copy.start()
    ranks_copy.start()
    for n in range(PIX_CHUNKS):
        pix_copy(n).start()
    barrier = pltpu.get_barrier_semaphore()
    for row, col in peers:
        pl.semaphore_signal(barrier, inc=1, device_id={"row": row, "col": col}, device_id_type=MESH)

    lanes[...] = one_hot((256, 256), lambda row: (row & 127) * 2 + (row >> 7))
    slopes[...] = jnp.zeros_like(slopes)
    folds[...] = jnp.zeros_like(folds)

    filt_copy.wait()
    filt32[...] = filt[...].astype(F32)

    def centroid(n, carry):
        pix_copy(n).wait()
        for lane in range(4):
            low, high = lane * 128, min(lane * 128 + 128, SUBS)
            width = high - low

            zero = jnp.zeros((8, width), F32)
            sums = [[zero] * CHUNK_FRAMES for _ in range(3)]
            for p in range(0, PIX, 16):
                fx = filt32[0, p : p + 16, low:high]
                fy = filt32[1, p : p + 16, low:high]
                for f in range(CHUNK_FRAMES):
                    v = pix[n * CHUNK_FRAMES + f, p : p + 16, low:high].astype(F32)
                    vx, vy = v * fx, v * fy
                    sums[0][f] = sums[0][f] + (v[:8] + v[8:])
                    sums[1][f] = sums[1][f] + (vx[:8] + vx[8:])
                    sums[2][f] = sums[2][f] + (vy[:8] + vy[8:])
            for kind in range(3):
                for f in range(CHUNK_FRAMES):
                    first = (lane * 3 + kind) * 64 + f * 8
                    folds[first : first + 8, :width] = sums[kind][f]

            def total(kind):
                first = (lane * 3 + kind) * 64
                return sum(folds[pl.ds(first + k, CHUNK_FRAMES, stride=8), :] for k in range(8))[:, :width]

            flux = total(0)
            frames = pl.ds(pl.multiple_of(n * CHUNK_FRAMES, 8), CHUNK_FRAMES)
            slopes[0, frames, low:high] = total(1) / flux
            slopes[1, frames, low:high] = total(2) / flux
        return carry

    lax.fori_loop(0, PIX_CHUNKS, centroid, 0)

    parts = []
    for b in range(2):
        kinds = [slopes[k] if b == 0 else pltpu.roll(slopes[k], 512 - HALF, 1) for k in range(2)]
        for h in range(2):
            parts.append(jnp.concatenate([v[:, h * 128 : h * 128 + 128] for v in kinds], axis=1))
    raw = jnp.concatenate(parts, axis=0).astype(BF16)
    raw = jnp.dot(raw, lanes[...], preferred_element_type=F32)

    for b in range(2):
        for h in range(2):
            for q in range(2):
                first = b * 128 + h * 64
                rows32[pl.ds(h * 8 + b * 2 + q, FRAMES, stride=16), :] = raw[
                    first : first + FRAMES, q * 128 : q * 128 + 128
                ]
    by_piece[...] = rows32[...].reshape(DEVICES, 8, 128).astype(BF16)

    pl.semaphore_wait(barrier, DEVICES - 1)

    def remote(src, dst, send, recv, device):
        return pltpu.make_async_remote_copy(
            src_ref=src, dst_ref=dst, send_sem=send, recv_sem=recv, device_id=device, device_id_type=MESH
        )

    for row, col in peers:
        remote(
            by_piece.at[row * COLS + col, pl.ds(0, 4)], at_mid.at[rank, pl.ds(0, 4)], spread_send, spread_recv, {"row": row, "col": col}
        ).start()
    at_mid[rank] = by_piece[rank]
    order_copy.wait()
    wanted = jnp.broadcast_to(order[...].astype(F32), (128, 256)).T
    source = lax.broadcasted_iota(jnp.int32, (256, 128), 1)
    for b in range(2):
        match = (source * 2 + b).astype(F32) == wanted
        sel[:, b * 128 : b * 128 + 128] = jnp.where(match, 1.0, 0.0).astype(BF16)
    frame_rows[...] = one_hot((256, 256), lambda row: (row & 31) * 8 + (row >> 5))
    for n in range(R_CHUNKS):
        right_copy(n).start()
    others = pl.ds(0, DEVICES - 1)
    spread = remote(by_piece.at[others, pl.ds(0, 4)], at_mid.at[others, pl.ds(0, 4)], spread_send, spread_recv, {"row": r})
    spread.wait_recv()
    rows32[...] = at_mid[...].astype(F32).reshape(DEVICES * 8, 128)
    every = jnp.concatenate(
        [
            jnp.concatenate([rows32[pl.ds(b * 2 + q, DEVICES, stride=8), :] for q in range(2)], axis=1)
            for b in range(2)
        ],
        axis=0,
    ).astype(BF16)
    chosen = jnp.dot(sel[...], every, preferred_element_type=F32).reshape(COLS, 2, SPAN_J // 2, 256)
    for part in range(2):
        by_col[part] = chosen[:, part].astype(BF16)

    def gather_to(part, dx):
        for row, col in peers_at[dx]:
            remote(
                by_col.at[part, col], gathered.at[part, rank], gather_send.at[part, dx], gather_recv.at[part, dx],
                {"row": row, "col": col},
            ).start()

    def gathered_at(part, dx):
        slots = pl.ds(0, len(peers_at[dx]))
        return remote(
            gathered.at[part, slots], gathered.at[part, slots], gather_send.at[part, dx], gather_recv.at[part, dx],
            {"row": r},
        )

    def relay(part):
        slots = pl.ds(xs[3 if part == 0 else 1] * 32, 32)
        return remote(
            gathered.at[part, slots], gathered.at[part, slots], gather_send.at[part, 2], gather_recv.at[part, 2],
            {"row": xs[1 if part == 0 else 3] * 2 + lax.rem(r, 2), "col": c},
        )

    gather_to(0, 1)
    gather_to(1, 3)
    gather_to(0, 3)
    gather_to(0, 0)
    gathered[0, rank] = by_col[0, c]
    gather_to(1, 1)
    gathered_at(0, 1).wait_recv()
    relay(0).start()
    gather_to(1, 0)
    gathered[1, rank] = by_col[1, c]
    gathered_at(1, 3).wait_recv()
    relay(1).start()
    for n in range(SPAN_I):
        left_copy(n).start()
    ranks_copy.wait()

    def arrive(part):
        right_copy(2 * part).wait()
        right_copy(2 * part + 1).wait()
        gathered_at(part, 3 if part == 0 else 1).wait_recv()
        gathered_at(part, 0).wait_recv()
        relay(part).wait_recv()
        for g in range(2):
            for h in range(2):
                rows = jnp.concatenate(
                    [gathered[part, 2 * (g * 32 + f) + h].astype(F32) for f in range(32)], axis=0
                ).astype(BF16)
                pieces[part * 8 : part * 8 + 8, g * 32 : g * 32 + 32, h * 256 : h * 256 + 256] = permute(
                    frame_rows[...], rows
                ).reshape(SPAN_J // 2, 32, 256)

    lane_id = lax.broadcasted_iota(jnp.int32, (FRAMES, 128), 1)
    low_half = lane_id < RANK
    component = lane_id & (RANK - 1)

    def project(n, first):
        for q in range(CHUNK_PAIRS):
            pair = n * CHUNK_PAIRS + q
            halves = []
            for e in range(2):
                factors = right[pl.ds(first, 4), 2 * pair + e].reshape(4 * RANK, TILE)
                halves.append(
                    lax.dot_general(
                        pieces[2 * pair + e][:, :TILE], factors, (((1,), (1,)), ((), ())), preferred_element_type=F32
                    )
                )
            for i2 in range(2):
                i = first + 2 * i2
                kept = []
                for e in range(2):
                    bound = jnp.where(low_half, ranks[i, 2 * pair + e], ranks[i + 1, 2 * pair + e])
                    kept.append(jnp.where(component < bound, halves[e][:, i2 * 128 : i2 * 128 + 128], 0.0))
                proj[i, pair] = jnp.where(low_half, kept[0], pltpu.roll(kept[1], RANK, 1)).astype(BF16)
                proj[i + 1, pair] = jnp.where(low_half, pltpu.roll(kept[0], RANK, 1), kept[1]).astype(BF16)

    def tile_product(i, start, stop):
        lhs = jnp.concatenate([proj[i, q] for q in range(start, stop)], axis=1)
        factors = left[i, 2 * start : 2 * stop].reshape(2 * (stop - start) * RANK, TILE)
        return jnp.dot(lhs, factors, preferred_element_type=F32)

    far, near = (1 - z_hi) * 4, z_hi * 4
    arrive(0)
    project(0, far)
    project(1, far)
    for n in range(SPAN_I):
        left_copy(n).wait()
    for k in range(4):
        early[k] = tile_product(far + k, 0, PAIRS // 2)
    arrive(1)

    def half_copy(s):
        return remote(
            other_half.at[s], half_in.at[s], c1_send.at[s], c1_recv.at[s], {"row": r, "col": c + 1 - 2 * core}
        )

    def tile_of(s):
        return lax.rem(z_hi + 1 - s // 4, 2) * 4 + ys[(2, 1, 3, 0)[s % 4]]

    def chunk_copy(s):
        return remote(
            chunk_out.at[s], chunk_in.at[s], c2_send.at[s], c2_recv.at[s], {"row": r, "col": 2 * tile_of(s) + core}
        )

    def direct_copy():
        return remote(
            direct_out, direct_in, direct_send, direct_recv, {"row": r, "col": 2 * tile_of(6) + 1 - core}
        )

    def finish(s):
        half_copy(s).wait_recv()
        chunk_out[s] = (my_half[s] + half_in[s]).astype(BF16)
        chunk_copy(s).start()

    def commands(steps):
        full = []
        for s in steps:
            i = tile_of(s)
            if s < 4:
                full.append(early[i - far] + tile_product(i, PAIRS // 2, PAIRS))
            else:
                full.append(tile_product(i, 0, PAIRS))
        first = core == 0
        for s, tile in zip(steps, full):
            lower, upper = tile[:, :HALF], tile[:, HALF:]
            other_half[s] = jnp.where(first, upper, lower)
            my_half[s] = jnp.where(first, lower, upper)
            if s == 6:
                chunk_out[s] = my_half[s].astype(BF16)
                chunk_copy(s).start()
                direct_out[...] = other_half[s].astype(BF16)
                direct_copy().start()
            else:
                half_copy(s).start()

    project(2, far)
    project(3, far)
    commands((0, 1))
    commands((2, 3))
    project(0, near)
    finish(0)
    finish(1)
    project(1, near)
    finish(2)
    finish(3)
    project(2, near)
    project(3, near)
    commands((4, 5))
    commands((6, 7))
    finish(4)
    finish(5)
    last = SPAN_I - 1
    half_copy(last).wait_recv()
    total_cmd = my_half[last] + half_in[last]
    for s in range(last):
        chunk_copy(s).wait_recv()
        total_cmd += chunk_in[s].astype(F32)
    direct_copy().wait_recv()
    total_cmd += direct_in[...].astype(F32)
    out_ref[...] = total_cmd

    spread.wait_send()
    for part in range(2):
        for dx in (0, 1, 3):
            gathered_at(part, dx).wait_send()
        relay(part).wait_send()
    for s in (0, 1, 2, 3, 4, 5, 7):
        half_copy(s).wait_send()
    direct_copy().wait_send()
    for s in range(last):
        chunk_copy(s).wait_send()


def shards(pixels, match_filter, tile_ranks, column_order, right_factors, left_factors):
    hbm = pl.BlockSpec(memory_space=pltpu.HBM)
    dma = pltpu.SemaphoreType.DMA
    return pl.pallas_call(
        kernel,
        out_shape=jax.ShapeDtypeStruct((FRAMES, HALF), F32),
        in_specs=[hbm] * 6,
        out_specs=pl.BlockSpec(memory_space=pltpu.VMEM),
        scratch_shapes=[
            pltpu.VMEM((1, 256), jnp.int32),
            pltpu.SMEM((SPAN_I, SPAN_J), jnp.int32),
            pltpu.VMEM((FRAMES, PIX, SUBS), BF16),
            pltpu.VMEM((2, PIX, SUBS), BF16),
            pltpu.VMEM((2, PIX, SUBS), F32),
            pltpu.VMEM((SPAN_I, SPAN_J, RANK, TILE), BF16),
            pltpu.VMEM((SPAN_I, SPAN_J, RANK, TILE), BF16),
            pltpu.VMEM((2, FRAMES, 512), F32),
            pltpu.VMEM((256, 256), BF16),
            pltpu.VMEM((256, 256), BF16),
            pltpu.VMEM((256, 256), BF16),
            pltpu.VMEM((DEVICES * 8, 128), F32),
            pltpu.VMEM((4 * 3 * 64, 128), F32),
            pltpu.VMEM((DEVICES, 8, 128), BF16),
            pltpu.VMEM((DEVICES, 8, 128), BF16),
            pltpu.VMEM((2, COLS, SPAN_J // 2, 256), BF16),
            pltpu.VMEM((2, DEVICES, SPAN_J // 2, 256), BF16),
            pltpu.VMEM((SPAN_J, FRAMES, 512), BF16),
            pltpu.VMEM((SPAN_I, PAIRS, FRAMES, 128), BF16),
            pltpu.VMEM((SPAN_I, FRAMES, HALF), F32),
            pltpu.VMEM((SPAN_I, FRAMES, HALF), F32),
            pltpu.VMEM((4, FRAMES, TILE), F32),
            pltpu.VMEM((SPAN_I, FRAMES, HALF), F32),
            pltpu.VMEM((SPAN_I - 1, FRAMES, HALF), BF16),
            pltpu.VMEM((SPAN_I - 1, FRAMES, HALF), BF16),
            pltpu.VMEM((FRAMES, HALF), BF16),
            pltpu.VMEM((FRAMES, HALF), BF16),
            dma, dma, dma, dma((PIX_CHUNKS,)), dma((R_CHUNKS,)), dma((SPAN_I,)),
            dma, dma, dma((2, 4)), dma((2, 4)),
            dma((SPAN_I,)), dma((SPAN_I,)),
            dma((SPAN_I - 1,)), dma((SPAN_I - 1,)), dma, dma,
        ],
        compiler_params=pltpu.CompilerParams(
            collective_id=0, has_side_effects=True, vmem_limit_bytes=64 * 1024 * 1024 - 65536
        ),
        name="frames_to_commands",
    )(
        column_order.reshape(1, -1),
        tile_ranks,
        jnp.transpose(pixels, (0, 2, 1)),
        jnp.transpose(match_filter, (1, 2, 0)),
        right_factors,
        left_factors,
    )


def solution(mesh):
    in_specs = (
        P(None, ("row", "col"), None),
        P(("row", "col"), None, None),
        P("row", "col"),
        P(),
        P("row", "col", None, None),
        P("row", "col", None, None),
    )
    out_specs = P(None, ("row", "col"))
    return jax.shard_map(shards, mesh=mesh, in_specs=in_specs, out_specs=out_specs, check_vma=False)
```

```python
import jax
import jax.numpy as jnp
from jax import lax
from jax.experimental import pallas as pl
from jax.experimental.pallas import tpu as pltpu
from jax.sharding import PartitionSpec as P

BF16 = jnp.bfloat16
F32 = jnp.float32
ROWS, COLS = 8, 16
FRAMES, SUBS, PIX = 64, 500, 144
TILE, RANK = 500, 64
SPAN_I, SPAN_J = 8, 16
HALF = 250
PIX_CHUNKS = 8
CHUNK_FRAMES = FRAMES // PIX_CHUNKS
R_CHUNKS = 4
R_COLS = SPAN_J // R_CHUNKS
PAIRS = SPAN_J // 2
CHUNK_PAIRS = PAIRS // R_CHUNKS
DEVICES = ROWS * COLS
MESH = pl.DeviceIdType.MESH


def one_hot(shape, target_of_row):
    row = lax.broadcasted_iota(jnp.int32, shape, 0)
    col = lax.broadcasted_iota(jnp.int32, shape, 1)
    return jnp.where(col == target_of_row(row), 1.0, 0.0).astype(BF16)


def permute(matrix, rows):
    return jnp.dot(matrix, rows, preferred_element_type=F32).astype(BF16)


def kernel(
    order_hbm, ranks_hbm, pix_hbm, filt_hbm, right_hbm, left_hbm, out_ref,
    order, ranks, pix, filt, filt32, right, left, slopes, sel, lanes, frame_rows, rows32, folds, by_piece, at_mid, by_col, gathered,
    pieces, proj, other_half, my_half, early, half_in, chunk_out, chunk_in, direct_out, direct_in,
    order_sem, ranks_sem, filt_sem, pix_sem, right_sem, left_sem,
    spread_send, spread_recv, gather_send, gather_recv,
    c1_send, c1_recv, c2_send, c2_recv, direct_send, direct_recv,
):
    r = lax.axis_index("row")
    c = lax.axis_index("col")
    core = lax.rem(c, 2)
    y = lax.rem(c // 2, 4)
    z_hi = c // 8
    x = r // 2
    z = z_hi * 2 + lax.rem(r, 2)
    rank = r * COLS + c

    xs = [lax.rem(x + d, 4) for d in range(4)]
    ys = [lax.rem(y + d, 4) for d in range(4)]
    zs = [lax.rem(z + d, 4) for d in range(4)]
    cores = [core, 1 - core]
    offsets = [(dx, dy, dz, dk) for dx in range(4) for dy in range(4) for dz in range(4) for dk in range(2)]
    offsets.sort(key=lambda o: -sum(min(d, 4 - d) for d in o[:3]))
    peers_at = {d: [] for d in range(4)}
    peers = []
    for dx, dy, dz, dk in offsets:
        if (dx, dy, dz, dk) != (0, 0, 0, 0):
            peer = (xs[dx] * 2 + lax.rem(zs[dz], 2), (zs[dz] // 2 * 4 + ys[dy]) * 2 + cores[dk])
            peers.append(peer)
            peers_at[dx].append(peer)

    def pix_copy(n):
        frames = pl.ds(n * CHUNK_FRAMES, CHUNK_FRAMES)
        return pltpu.make_async_copy(pix_hbm.at[frames], pix.at[frames], pix_sem.at[n])

    def right_copy(n):
        cols = pl.ds(n * R_COLS, R_COLS)
        return pltpu.make_async_copy(right_hbm.at[:, cols], right.at[:, cols], right_sem.at[n])

    def left_copy(n):
        return pltpu.make_async_copy(left_hbm.at[n], left.at[n], left_sem.at[n])

    order_copy = pltpu.make_async_copy(order_hbm, order, order_sem)
    ranks_copy = pltpu.make_async_copy(ranks_hbm, ranks, ranks_sem)
    filt_copy = pltpu.make_async_copy(filt_hbm, filt, filt_sem)
    filt_copy.start()
    order_copy.start()
    ranks_copy.start()
    for n in range(PIX_CHUNKS):
        pix_copy(n).start()
    barrier = pltpu.get_barrier_semaphore()
    for row, col in peers:
        pl.semaphore_signal(barrier, inc=1, device_id={"row": row, "col": col}, device_id_type=MESH)

    lanes[...] = one_hot((256, 256), lambda row: (row & 127) * 2 + (row >> 7))
    slopes[...] = jnp.zeros_like(slopes)
    folds[...] = jnp.zeros_like(folds)

    filt_copy.wait()
    filt32[...] = filt[...].astype(F32)

    def centroid(n, carry):
        pix_copy(n).wait()
        for lane in range(4):
            low, high = lane * 128, min(lane * 128 + 128, SUBS)
            width = high - low

            zero = jnp.zeros((8, width), F32)
            sums = [[zero] * CHUNK_FRAMES for _ in range(3)]
            for p in range(0, PIX, 16):
                fx = filt32[0, p : p + 16, low:high]
                fy = filt32[1, p : p + 16, low:high]
                for f in range(CHUNK_FRAMES):
                    v = pix[n * CHUNK_FRAMES + f, p : p + 16, low:high].astype(F32)
                    vx, vy = v * fx, v * fy
                    sums[0][f] = sums[0][f] + (v[:8] + v[8:])
                    sums[1][f] = sums[1][f] + (vx[:8] + vx[8:])
                    sums[2][f] = sums[2][f] + (vy[:8] + vy[8:])
            for kind in range(3):
                for f in range(CHUNK_FRAMES):
                    first = (lane * 3 + kind) * 64 + f * 8
                    folds[first : first + 8, :width] = sums[kind][f]

            def total(kind):
                first = (lane * 3 + kind) * 64
                return sum(folds[pl.ds(first + k, CHUNK_FRAMES, stride=8), :] for k in range(8))[:, :width]

            flux = total(0)
            frames = pl.ds(pl.multiple_of(n * CHUNK_FRAMES, 8), CHUNK_FRAMES)
            slopes[0, frames, low:high] = total(1) / flux
            slopes[1, frames, low:high] = total(2) / flux
        return carry

    lax.fori_loop(0, PIX_CHUNKS, centroid, 0)

    parts = []
    for b in range(2):
        kinds = [slopes[k] if b == 0 else pltpu.roll(slopes[k], 512 - HALF, 1) for k in range(2)]
        for h in range(2):
            parts.append(jnp.concatenate([v[:, h * 128 : h * 128 + 128] for v in kinds], axis=1))
    raw = jnp.concatenate(parts, axis=0).astype(BF16)
    raw = jnp.dot(raw, lanes[...], preferred_element_type=F32)

    for b in range(2):
        for h in range(2):
            for q in range(2):
                first = b * 128 + h * 64
                rows32[pl.ds(h * 8 + b * 2 + q, FRAMES, stride=16), :] = raw[
                    first : first + FRAMES, q * 128 : q * 128 + 128
                ]
    by_piece[...] = rows32[...].reshape(DEVICES, 8, 128).astype(BF16)

    pl.semaphore_wait(barrier, DEVICES - 1)

    def remote(src, dst, send, recv, device):
        return pltpu.make_async_remote_copy(
            src_ref=src, dst_ref=dst, send_sem=send, recv_sem=recv, device_id=device, device_id_type=MESH
        )

    for row, col in peers:
        remote(
            by_piece.at[row * COLS + col, pl.ds(0, 4)], at_mid.at[rank, pl.ds(0, 4)], spread_send, spread_recv, {"row": row, "col": col}
        ).start()
    at_mid[rank] = by_piece[rank]
    order_copy.wait()
    wanted = jnp.broadcast_to(order[...].astype(F32), (128, 256)).T
    source = lax.broadcasted_iota(jnp.int32, (256, 128), 1)
    for b in range(2):
        match = (source * 2 + b).astype(F32) == wanted
        sel[:, b * 128 : b * 128 + 128] = jnp.where(match, 1.0, 0.0).astype(BF16)
    frame_rows[...] = one_hot((256, 256), lambda row: (row & 31) * 8 + (row >> 5))
    for n in range(R_CHUNKS):
        right_copy(n).start()
    others = pl.ds(0, DEVICES - 1)
    spread = remote(by_piece.at[others, pl.ds(0, 4)], at_mid.at[others, pl.ds(0, 4)], spread_send, spread_recv, {"row": r})
    spread.wait_recv()
    rows32[...] = at_mid[...].astype(F32).reshape(DEVICES * 8, 128)
    every = jnp.concatenate(
        [
            jnp.concatenate([rows32[pl.ds(b * 2 + q, DEVICES, stride=8), :] for q in range(2)], axis=1)
            for b in range(2)
        ],
        axis=0,
    ).astype(BF16)
    chosen = jnp.dot(sel[...], every, preferred_element_type=F32).reshape(COLS, 2, SPAN_J // 2, 256)
    for part in range(2):
        by_col[part] = chosen[:, part].astype(BF16)

    def gather_to(part, dx):
        for row, col in peers_at[dx]:
            remote(
                by_col.at[part, col], gathered.at[part, rank], gather_send.at[part, dx], gather_recv.at[part, dx],
                {"row": row, "col": col},
            ).start()

    def gathered_at(part, dx):
        slots = pl.ds(0, len(peers_at[dx]))
        return remote(
            gathered.at[part, slots], gathered.at[part, slots], gather_send.at[part, dx], gather_recv.at[part, dx],
            {"row": r},
        )

    def relay(part):
        slots = pl.ds(xs[3 if part == 0 else 1] * 32, 32)
        return remote(
            gathered.at[part, slots], gathered.at[part, slots], gather_send.at[part, 2], gather_recv.at[part, 2],
            {"row": xs[1 if part == 0 else 3] * 2 + lax.rem(r, 2), "col": c},
        )

    gather_to(0, 1)
    gather_to(1, 3)
    gather_to(0, 3)
    gather_to(0, 0)
    gathered[0, rank] = by_col[0, c]
    gather_to(1, 1)
    gathered_at(0, 1).wait_recv()
    relay(0).start()
    gather_to(1, 0)
    gathered[1, rank] = by_col[1, c]
    gathered_at(1, 3).wait_recv()
    relay(1).start()
    for n in range(SPAN_I):
        left_copy(n).start()
    ranks_copy.wait()

    def arrive(part):
        right_copy(2 * part).wait()
        right_copy(2 * part + 1).wait()
        gathered_at(part, 3 if part == 0 else 1).wait_recv()
        gathered_at(part, 0).wait_recv()
        relay(part).wait_recv()
        for g in range(2):
            for h in range(2):
                rows = jnp.concatenate(
                    [gathered[part, 2 * (g * 32 + f) + h].astype(F32) for f in range(32)], axis=0
                ).astype(BF16)
                pieces[part * 8 : part * 8 + 8, g * 32 : g * 32 + 32, h * 256 : h * 256 + 256] = permute(
                    frame_rows[...], rows
                ).reshape(SPAN_J // 2, 32, 256)

    lane_id = lax.broadcasted_iota(jnp.int32, (FRAMES, 128), 1)
    low_half = lane_id < RANK
    component = lane_id & (RANK - 1)

    def project(n, first):
        for q in range(CHUNK_PAIRS):
            pair = n * CHUNK_PAIRS + q
            halves = []
            for e in range(2):
                factors = right[pl.ds(first, 4), 2 * pair + e].reshape(4 * RANK, TILE)
                halves.append(
                    lax.dot_general(
                        pieces[2 * pair + e][:, :TILE], factors, (((1,), (1,)), ((), ())), preferred_element_type=F32
                    )
                )
            for i2 in range(2):
                i = first + 2 * i2
                kept = []
                for e in range(2):
                    bound = jnp.where(low_half, ranks[i, 2 * pair + e], ranks[i + 1, 2 * pair + e])
                    kept.append(jnp.where(component < bound, halves[e][:, i2 * 128 : i2 * 128 + 128], 0.0))
                proj[i, pair] = jnp.where(low_half, kept[0], pltpu.roll(kept[1], RANK, 1)).astype(BF16)
                proj[i + 1, pair] = jnp.where(low_half, pltpu.roll(kept[0], RANK, 1), kept[1]).astype(BF16)

    def tile_product(i, start, stop):
        lhs = jnp.concatenate([proj[i, q] for q in range(start, stop)], axis=1)
        factors = left[i, 2 * start : 2 * stop].reshape(2 * (stop - start) * RANK, TILE)
        return jnp.dot(lhs, factors, preferred_element_type=F32)

    far, near = (1 - z_hi) * 4, z_hi * 4
    arrive(0)
    project(0, far)
    project(1, far)
    for n in range(SPAN_I):
        left_copy(n).wait()
    for k in range(4):
        early[k] = tile_product(far + k, 0, PAIRS // 2)
    project(0, near)
    project(1, near)
    arrive(1)

    def half_copy(s):
        return remote(
            other_half.at[s], half_in.at[s], c1_send.at[s], c1_recv.at[s], {"row": r, "col": c + 1 - 2 * core}
        )

    def tile_of(s):
        return lax.rem(z_hi + 1 - s // 4, 2) * 4 + ys[(2, 1, 3, 0)[s % 4]]

    def chunk_copy(s):
        return remote(
            chunk_out.at[s], chunk_in.at[s], c2_send.at[s], c2_recv.at[s], {"row": r, "col": 2 * tile_of(s) + core}
        )

    def direct_copy():
        return remote(
            direct_out, direct_in, direct_send, direct_recv, {"row": r, "col": 2 * tile_of(6) + 1 - core}
        )

    def finish(s):
        half_copy(s).wait_recv()
        chunk_out[s] = (my_half[s] + half_in[s]).astype(BF16)
        chunk_copy(s).start()

    def commands(steps):
        full = []
        for s in steps:
            i = tile_of(s)
            if s < 4:
                full.append(early[i - far] + tile_product(i, PAIRS // 2, PAIRS))
            else:
                full.append(tile_product(i, 0, PAIRS))
        first = core == 0
        for s, tile in zip(steps, full):
            lower, upper = tile[:, :HALF], tile[:, HALF:]
            other_half[s] = jnp.where(first, upper, lower)
            my_half[s] = jnp.where(first, lower, upper)
            if s == 6:
                chunk_out[s] = my_half[s].astype(BF16)
                chunk_copy(s).start()
                direct_out[...] = other_half[s].astype(BF16)
                direct_copy().start()
            else:
                half_copy(s).start()

    project(2, far)
    project(3, far)
    commands((0, 1))
    commands((2, 3))
    project(2, near)
    finish(0)
    finish(1)
    project(3, near)
    finish(2)
    finish(3)
    commands((4, 5))
    commands((6, 7))
    finish(4)
    finish(5)
    last = SPAN_I - 1
    half_copy(last).wait_recv()
    total_cmd = my_half[last] + half_in[last]
    for s in range(last):
        chunk_copy(s).wait_recv()
        total_cmd += chunk_in[s].astype(F32)
    direct_copy().wait_recv()
    total_cmd += direct_in[...].astype(F32)
    out_ref[...] = total_cmd

    spread.wait_send()
    for part in range(2):
        for dx in (0, 1, 3):
            gathered_at(part, dx).wait_send()
        relay(part).wait_send()
    for s in (0, 1, 2, 3, 4, 5, 7):
        half_copy(s).wait_send()
    direct_copy().wait_send()
    for s in range(last):
        chunk_copy(s).wait_send()


def shards(pixels, match_filter, tile_ranks, column_order, right_factors, left_factors):
    hbm = pl.BlockSpec(memory_space=pltpu.HBM)
    dma = pltpu.SemaphoreType.DMA
    return pl.pallas_call(
        kernel,
        out_shape=jax.ShapeDtypeStruct((FRAMES, HALF), F32),
        in_specs=[hbm] * 6,
        out_specs=pl.BlockSpec(memory_space=pltpu.VMEM),
        scratch_shapes=[
            pltpu.VMEM((1, 256), jnp.int32),
            pltpu.SMEM((SPAN_I, SPAN_J), jnp.int32),
            pltpu.VMEM((FRAMES, PIX, SUBS), BF16),
            pltpu.VMEM((2, PIX, SUBS), BF16),
            pltpu.VMEM((2, PIX, SUBS), F32),
            pltpu.VMEM((SPAN_I, SPAN_J, RANK, TILE), BF16),
            pltpu.VMEM((SPAN_I, SPAN_J, RANK, TILE), BF16),
            pltpu.VMEM((2, FRAMES, 512), F32),
            pltpu.VMEM((256, 256), BF16),
            pltpu.VMEM((256, 256), BF16),
            pltpu.VMEM((256, 256), BF16),
            pltpu.VMEM((DEVICES * 8, 128), F32),
            pltpu.VMEM((4 * 3 * 64, 128), F32),
            pltpu.VMEM((DEVICES, 8, 128), BF16),
            pltpu.VMEM((DEVICES, 8, 128), BF16),
            pltpu.VMEM((2, COLS, SPAN_J // 2, 256), BF16),
            pltpu.VMEM((2, DEVICES, SPAN_J // 2, 256), BF16),
            pltpu.VMEM((SPAN_J, FRAMES, 512), BF16),
            pltpu.VMEM((SPAN_I, PAIRS, FRAMES, 128), BF16),
            pltpu.VMEM((SPAN_I, FRAMES, HALF), F32),
            pltpu.VMEM((SPAN_I, FRAMES, HALF), F32),
            pltpu.VMEM((4, FRAMES, TILE), F32),
            pltpu.VMEM((SPAN_I, FRAMES, HALF), F32),
            pltpu.VMEM((SPAN_I - 1, FRAMES, HALF), BF16),
            pltpu.VMEM((SPAN_I - 1, FRAMES, HALF), BF16),
            pltpu.VMEM((FRAMES, HALF), BF16),
            pltpu.VMEM((FRAMES, HALF), BF16),
            dma, dma, dma, dma((PIX_CHUNKS,)), dma((R_CHUNKS,)), dma((SPAN_I,)),
            dma, dma, dma((2, 4)), dma((2, 4)),
            dma((SPAN_I,)), dma((SPAN_I,)),
            dma((SPAN_I - 1,)), dma((SPAN_I - 1,)), dma, dma,
        ],
        compiler_params=pltpu.CompilerParams(
            collective_id=0, has_side_effects=True, vmem_limit_bytes=64 * 1024 * 1024 - 65536
        ),
        name="frames_to_commands",
    )(
        column_order.reshape(1, -1),
        tile_ranks,
        jnp.transpose(pixels, (0, 2, 1)),
        jnp.transpose(match_filter, (1, 2, 0)),
        right_factors,
        left_factors,
    )


def solution(mesh):
    in_specs = (
        P(None, ("row", "col"), None),
        P(("row", "col"), None, None),
        P("row", "col"),
        P(),
        P("row", "col", None, None),
        P("row", "col", None, None),
    )
    out_specs = P(None, ("row", "col"))
    return jax.shard_map(shards, mesh=mesh, in_specs=in_specs, out_specs=out_specs, check_vma=False)
```
